32 devices in a mesh: pat: 8 (over y, x, core), code: 4 (over z).
Axes of the slice: x: 2, y: 2, z: 4, core: 2. Of those that a mesh axis runs over, the one named last changes fastest.
Arguments:
- tile_data: bfloat16 [8, 4, 16, 128, 512], P('pat', 'code'), may hold values from 0 to 7, as said below
- tile_list: int32 [8, 4, 3, 16], P('pat', 'code'), may hold values from 0 to 31, as said below
- tile_count: int32 [8, 4], P('pat', 'code'), may hold values from 8 to 16, as said below
- visit_counts: int32 [128], P('pat'), may hold values from 1 to 256, as said below
- code_factor_t: float32 [64, 65536], P(None, 'code'), may hold values from 0.004 to 0.33, as said below
- visit_mix: float32 [64, 64], replicated, may hold values from -0.15 to 1.2
- patient_weight: float32 [128, 64], P('pat'), may hold values from 0.5 to 30, as said below
Outputs:
- code_factor_new: float32 [64, 65536], P(None, 'code')
- mix_new: float32 [64, 64], replicated
- patient_weight_new: float32 [128, 64], P(('pat', 'code'))
The draws below stay inside these ranges and needn't reach their ends.
Inputs may be any that keep to these rules, and one draw needn't show every extreme that they name: `tile_list`: for device (p, c) and slot t: entry 0 is a patient of pat index p (0 to 15), entry 1 a visit block below that patient's visits divided by 128 and rounded up, entry 2 a code block of code index c (0 to 31). A triple may repeat; such tiles add. `tile_count`: slots at or past a device's count are not in use; some device uses all slots. `visit_counts`: some patient has 256 visits. `tile_data`: Whole-number counts. Rows past the patient's visit count and slots not in use hold left-over values that are not part of the data. `code_factor_t`: Positive. `patient_weight`: Positive.
All inputs are finite; a program needn't handle non-finite values.
Results may differ from the reference program's by a relative error of at most 0.0073.
Values may be sent and summed in bfloat16 or wider, within the bound.
A program may use at most 64 MiB of HBM per device.

```python
import jax
import jax.numpy as jnp
from jax import lax

RANK = 64
CODES = 65536
TILE_V = 128
TILE_C = 512
VBLOCKS = 2
NS_STEPS = 8
TILES_DEV = 16
PAT_ROW = 16
PATIENTS = 128
CB_DEV = 32
VMAX = 256
N_PAT = 8
N_CODE = 4


def visit_helper(key):
    base_counts = jax.random.randint(jax.random.fold_in(key, 11), (PATIENTS,), 1, VMAX + 1)
    chosen = jax.random.randint(jax.random.fold_in(key, 12), (), 0, PATIENTS)
    return jnp.where(jnp.arange(PATIENTS) == chosen, VMAX, base_counts).astype(jnp.int32)


def draw_visit_counts(key, part):
    return visit_helper(key)


def draw_tile_list(key, part):
    visits = visit_helper(key)
    shape_all = (N_PAT, N_CODE, TILES_DEV)
    owners = jax.random.randint(jax.random.fold_in(key, 21), shape_all, 0, PAT_ROW)
    global_owner = owners + (jnp.arange(N_PAT) * PAT_ROW)[:, None, None]
    block_limit = (visits[global_owner] + TILE_V - 1) // TILE_V
    visit_block = jax.random.randint(jax.random.fold_in(key, 22), shape_all, 0, block_limit)
    code_block = jax.random.randint(jax.random.fold_in(key, 23), shape_all, 0, CB_DEV)
    return jnp.stack([owners, visit_block, code_block], axis=2).astype(jnp.int32)


def draw_tile_count(key, part):
    counts = jax.random.randint(jax.random.fold_in(key, 31), (N_PAT, N_CODE), TILES_DEV // 2, TILES_DEV + 1)
    chosen = jax.random.randint(jax.random.fold_in(key, 32), (), 0, N_PAT * N_CODE)
    flat_index = jnp.arange(N_PAT * N_CODE).reshape(N_PAT, N_CODE)
    return jnp.where(flat_index == chosen, TILES_DEV, counts).astype(jnp.int32)


def draw_tile_data(key, part):
    shape_all = (N_PAT, N_CODE, TILES_DEV, TILE_V, TILE_C)
    values = jax.random.randint(jax.random.fold_in(key, 41), shape_all, 0, 4)
    present = jax.random.randint(jax.random.fold_in(key, 42), shape_all, 0, 2) == 0
    return jnp.where(present, values, 0).astype(jnp.float32).astype(jnp.bfloat16)


def draw_code_factor_t(key, part):
    position = jnp.arange(CODES, dtype=jnp.float32) / CODES
    growth = 3.0 ** position
    base_values = jax.random.uniform(jax.random.fold_in(key, 51), (RANK, CODES), jnp.float32, 0.5, 1.5)
    return 0.02 * base_values * growth[None, :]


def draw_visit_mix(key, part):
    eye_mat = jnp.eye(RANK, dtype=jnp.float32)
    offdiag = jax.random.uniform(jax.random.fold_in(key, 61), (RANK, RANK), jnp.float32, -0.15, 0.15)
    diag_values = jax.random.uniform(jax.random.fold_in(key, 62), (RANK,), jnp.float32, 0.95, 1.05)
    return offdiag * (1.0 - eye_mat) + eye_mat * diag_values[None, :]


def draw_patient_weight(key, part):
    position = jnp.arange(PATIENTS, dtype=jnp.float32) / PATIENTS
    growth = 3.0 ** position
    base_values = jax.random.uniform(jax.random.fold_in(key, 71), (PATIENTS, RANK), jnp.float32, 0.5, 1.5)
    return base_values * growth[:, None]


def setup_inputs(seed: int = 0) -> dict:
    key_list = jax.random.split(jax.random.key(seed), 8)
    return {
        "tile_data": draw_tile_data(jax.random.fold_in(key_list[7], 71), 0),
        "tile_list": draw_tile_list(jax.random.fold_in(key_list[7], 71), 0),
        "tile_count": draw_tile_count(jax.random.fold_in(key_list[7], 71), 0),
        "visit_counts": draw_visit_counts(jax.random.fold_in(key_list[7], 71), 0),
        "code_factor_t": draw_code_factor_t(jax.random.fold_in(key_list[7], 71), 0),
        "visit_mix": draw_visit_mix(jax.random.fold_in(key_list[7], 71), 0),
        "patient_weight": draw_patient_weight(jax.random.fold_in(key_list[7], 71), 0),
    }


highest = lax.Precision.HIGHEST
damping = 0.1
epsilon = 1e-06

def damped_solve(gram, right):
    eye_mat = jnp.eye(gram.shape[0], dtype=gram.dtype)
    shifted = gram + damping * jnp.mean(jnp.diagonal(gram)) * eye_mat
    return jnp.linalg.solve(shifted, right)

def newton_schulz(target):
    norm_sq = lax.optimization_barrier(jnp.sum(target * target, axis=(1, 2, 3), keepdims=True))
    iterate = target / jnp.sqrt(norm_sq + epsilon)
    for step_number in range(NS_STEPS):
        inner_gram = jnp.einsum('kbrv,kbsv->krs', iterate, iterate, precision=highest)
        iterate = 1.5 * iterate - 0.5 * jnp.einsum('krs,kbsv->kbrv', inner_gram, iterate, precision=highest)
    return iterate

def keep_rows(owners, visit_block, live_count, visits_row, slot_total, tile_rows):
    match = owners[:, None] == jnp.arange(visits_row.shape[0], dtype=jnp.int32)[None, :]
    own_visits = lax.optimization_barrier(jnp.sum(jnp.where(match, visits_row[None, :], 0), axis=1))
    row_index = visit_block[:, None] * tile_rows + jnp.arange(tile_rows, dtype=jnp.int32)[None, :]
    in_use = jnp.arange(slot_total, dtype=jnp.int32) < live_count
    return (row_index < own_visits[:, None]) & in_use[:, None]

def reference(tile_data, tile_list, tile_count, visit_counts, code_factor_t, visit_mix, patient_weight):
    code_blocks = code_factor_t.astype(jnp.bfloat16).reshape(RANK, N_CODE * CB_DEV, TILE_C).astype(jnp.float32)
    segment_total = PAT_ROW * VBLOCKS

    def load_device(device_id):
        pat_at = device_id // N_CODE
        code_at = device_id % N_CODE
        tile_slab = tile_data[pat_at, code_at]
        listing = tile_list[pat_at, code_at]
        visits_row = lax.dynamic_slice_in_dim(visit_counts, pat_at * PAT_ROW, PAT_ROW, 0)
        keep_mask = keep_rows(listing[0], listing[1], tile_count[pat_at, code_at], visits_row, TILES_DEV, TILE_V)
        masked = jnp.where(keep_mask[:, :, None], tile_slab, jnp.zeros((), tile_slab.dtype)).astype(jnp.float32)
        return (pat_at, code_at, listing, masked)

    def gather_products(running, device_id):
        pat_at, code_at, listing, masked = load_device(device_id)
        picked = jnp.take(code_blocks, code_at * CB_DEV + listing[2], axis=1)
        contrib = jnp.einsum('rtc,tvc->trv', picked, masked, precision=highest)
        partial_value = jax.ops.segment_sum(contrib, listing[0] * VBLOCKS + listing[1], num_segments=segment_total)
        offset = pat_at * segment_total
        updated = lax.dynamic_slice_in_dim(running, offset, segment_total, 0) + partial_value
        return (lax.dynamic_update_slice_in_dim(running, updated, offset, 0), None)
    device_ids = jnp.arange(N_PAT * N_CODE, dtype=jnp.int32)
    flat_products, unused = lax.scan(gather_products, jnp.zeros((PATIENTS * VBLOCKS, RANK, TILE_V), jnp.float32), device_ids)
    products = flat_products.reshape(PATIENTS, VBLOCKS, RANK, TILE_V)
    code_gram = jnp.dot(code_factor_t, code_factor_t.T, precision=highest)
    target = jnp.einsum('rs,ks,kbsv->kbrv', visit_mix, patient_weight, products, precision=highest)
    polar_factor = newton_schulz(target)
    projected = jnp.einsum('kbrv,kbsv->krs', polar_factor, products, precision=highest)
    mix_numer = jnp.einsum('kis,ks->is', projected, patient_weight, precision=highest)
    weight_gram = jnp.dot(patient_weight.T, patient_weight, precision=highest)
    mix_new = damped_solve(code_gram * weight_gram, mix_numer.T).T
    mix_gram = jnp.dot(mix_new.T, mix_new, precision=highest)
    diag_terms = jnp.einsum('is,kis->ks', mix_new, projected, precision=highest)
    weight_new = jnp.maximum(damped_solve(mix_gram * code_gram, diag_terms.T).T, 0.0)
    spread = (jnp.einsum('is,kbiv->kbsv', mix_new, polar_factor, precision=highest) * weight_new[:, None, :, None]).astype(jnp.bfloat16)
    spread_flat = spread.reshape(PATIENTS * VBLOCKS, RANK, TILE_V).astype(jnp.float32)

    def gather_numer(running, device_id):
        pat_at, code_at, listing, masked = load_device(device_id)
        rows_used = (pat_at * PAT_ROW + listing[0]) * VBLOCKS + listing[1]
        picked = jnp.take(spread_flat, rows_used, axis=0)
        contrib = jnp.einsum('trv,tvc->trc', picked, masked, precision=highest)
        partial_value = jax.ops.segment_sum(contrib, listing[2], num_segments=CB_DEV)
        offset = code_at * CB_DEV
        updated = lax.dynamic_slice_in_dim(running, offset, CB_DEV, 1) + jnp.transpose(partial_value, (1, 0, 2))
        return (lax.dynamic_update_slice_in_dim(running, updated, offset, 1), None)
    numer_sums, unused = lax.scan(gather_numer, jnp.zeros((RANK, N_CODE * CB_DEV, TILE_C), jnp.float32), device_ids)
    weight_gram_new = jnp.dot(weight_new.T, weight_new, precision=highest)
    code_new = jnp.maximum(damped_solve(mix_gram * weight_gram_new, numer_sums.reshape(RANK, CODES)), 0.0)
    return (code_new, mix_new, weight_new)
```

```python
import functools

import jax
import jax.numpy as jnp
from jax import lax
from jax.experimental import pallas as pl
from jax.experimental.pallas import tpu as pltpu
from jax.sharding import PartitionSpec as P

VBLOCKS = 2
NS_STEPS = 8
INVERSE_STEPS = 8
MESH = pl.DeviceIdType.MESH
damping = 0.1
epsilon = 1e-06

f32 = jnp.float32
bf16 = jnp.bfloat16
VMEM = pl.BlockSpec(memory_space=pltpu.VMEM)
SMEM = pl.BlockSpec(memory_space=pltpu.SMEM)
LIMIT = 32 * 1024 * 1024


def mm(left, right, left_dim=1, right_dim=0):
    return lax.dot_general(
        left,
        right,
        (((left_dim,), (right_dim,)), ((), ())),
        precision=lax.Precision.HIGHEST,
        preferred_element_type=f32,
    )


def bmm(left, right, left_dim=1, right_dim=0):
    return lax.dot_general(
        left, right, (((left_dim,), (right_dim,)), ((), ())), preferred_element_type=f32
    )


def damped_inverse(gram):
    size = gram.shape[0]
    row_at = lax.broadcasted_iota(jnp.int32, (size, size), 0)
    lane_at = lax.broadcasted_iota(jnp.int32, (size, size), 1)
    eye = jnp.where(row_at == lane_at, 1.0, 0.0)
    trace = jnp.sum(jnp.sum(gram * eye, axis=1, keepdims=True), axis=0, keepdims=True)
    mean = trace * (1.0 / size)
    unscale = 1.0 / (mean * (0.5 * size + damping))
    a = gram * unscale + eye * (damping / (0.5 * size + damping))
    rest = eye - a
    tau = (size + 2.0 * damping) / size
    x = eye
    for step in range(INVERSE_STEPS):
        twice = 2.0 * tau * tau
        gain = twice / (twice - 1.0)
        if step == 0:
            x, square = x + rest, mm(rest, rest)
        else:
            both = mm(rest, jnp.concatenate([x, rest], axis=1))
            x, square = x + both[:, :size], both[:, size:]
        x = x * gain
        rest = square * gain - eye * (1.0 / (twice - 1.0))
        tau = twice - 1.0
    x = x + mm(x, eye - mm(a, x))
    return x * unscale


def live_rows(list_ref, count_ref, visits_ref, slot, tile_rows):
    owner, block, code = list_ref[0, 0, slot], list_ref[1, 0, slot], list_ref[2, 0, slot]
    limit = jnp.where(slot < count_ref[0], visits_ref[owner] - block * tile_rows, 0)
    return owner * VBLOCKS + block, code, limit


def products_kernel(list_ref, count_ref, visits_ref, tiles, factor, dev, col, gram, split, acc):
    slots, tile_rows, tile_cols = tiles.shape
    rank, codes = factor.shape
    step = min(2048, codes)
    total = jnp.zeros((2 * rank, 2 * rank), f32)
    profile = jnp.zeros((rank, 1), f32)
    for start in range(0, codes, step):
        part = factor[:, start : start + step]
        high = part.astype(bf16)
        split[:rank, start : start + step] = high
        split[rank:, start : start + step] = (part - high.astype(f32)).astype(bf16)
        profile += jnp.sum(part, axis=1, keepdims=True)
        both = split[:, start : start + step]
        total += bmm(both, both, 1, 1)
    profile = profile * (1.0 / codes)
    square = total[:rank, :rank] + total[:rank, rank:] + total[rank:, :rank] + total[rank:, rank:]
    both = jnp.concatenate([square, jnp.broadcast_to(profile, (rank, rank))], axis=1)
    rows = gram.shape[1]
    for p in range(gram.shape[0]):
        gram[p] = both[p * rows : (p + 1) * rows, :]
    acc[...] = jnp.zeros_like(acc)
    lane_at = lax.broadcasted_iota(jnp.int32, (rank, tile_rows), 1)
    for slot in range(slots):
        segment, code, limit = live_rows(list_ref, count_ref, visits_ref, slot, tile_rows)
        picked = split[:rank, pl.ds(pl.multiple_of(code * tile_cols, tile_cols), tile_cols)]
        contrib = bmm(picked, tiles[slot], 1, 1)
        acc[segment] += jnp.where(lane_at < limit, contrib, 0.0)
    whole = 1.0 / jnp.sum(profile, axis=0, keepdims=True)
    for segment in range(acc.shape[0]):
        value = acc[segment]
        column = jnp.sum(value, axis=0, keepdims=True) * whole
        col[segment : segment + 1, :] = column
        dev[segment] = (value - profile * column).astype(bf16)


def code_peer(me, distance, n_code):
    return lax.rem(me + distance, n_code)


def greet(n_pat, n_code, me_p, me_c):
    barrier = pltpu.get_barrier_semaphore()
    for d in range(1, n_code):
        pl.semaphore_signal(barrier, inc=1, device_id=(me_p, lax.rem(me_c + d, n_code)), device_id_type=MESH)
    for d in range(1, n_pat):
        pl.semaphore_signal(barrier, inc=1, device_id=(lax.rem(me_p + d, n_pat), me_c), device_id_type=MESH)
    pl.semaphore_wait(barrier, n_code + n_pat - 2)


def remote(src, dst, send, recv, where):
    copy = pltpu.make_async_remote_copy(
        src_ref=src, dst_ref=dst, send_sem=send, recv_sem=recv, device_id=where, device_id_type=MESH
    )
    copy.start()
    return copy


def exchange_kernel(
    n_pat, n_code, dev, col, gram, weight, dev_all, col_all, gram_all, weight_all, send_c, recv_c, send_p, recv_p, here
):
    me_p, me_c = lax.axis_index("pat"), lax.axis_index("code")
    own = dev.shape[0] // n_code
    greet(n_pat, n_code, me_p, me_c)
    copies = []
    for d in range(1, n_pat):
        copies.append(
            remote(weight, weight_all.at[me_p], send_p.at[0, d], recv_p.at[0, d], (lax.rem(me_p + d, n_pat), me_c))
        )
    rows = []
    for d in range(n_code - 1, 0, -1):
        to = lax.rem(me_c + d, n_code)
        where = (me_p, to)
        rows.append(
            remote(gram.at[me_p], gram_all.at[me_p, me_c], send_c.at[0, d], recv_c.at[0, d], where)
        )
    for d in range(n_code - 1, 0, -1):
        to = lax.rem(me_c + d, n_code)
        where = (me_p, to)
        copies.append(remote(col.at[pl.ds(to * own, own)], col_all.at[me_c], send_c.at[1, d], recv_c.at[1, d], where))
        copies.append(remote(dev.at[pl.ds(to * own, own)], dev_all.at[me_c], send_c.at[2, d], recv_c.at[2, d], where))
    local = [
        pltpu.make_async_copy(weight, weight_all.at[me_p], here.at[0]),
        pltpu.make_async_copy(gram.at[me_p], gram_all.at[me_p, me_c], here.at[1]),
        pltpu.make_async_copy(col.at[pl.ds(me_c * own, own)], col_all.at[me_c], here.at[2]),
        pltpu.make_async_copy(dev.at[pl.ds(me_c * own, own)], dev_all.at[me_c], here.at[3]),
    ]
    for copy in local:
        copy.start()
    for copy in local:
        copy.wait()
    for copy in rows:
        copy.wait_recv()
    slab = gram_all.at[me_p]
    for d in range(1, n_pat):
        copies.append(remote(slab, slab, send_p.at[1, d], recv_p.at[1, d], (lax.rem(me_p + d, n_pat), me_c)))
    for copy in copies:
        copy.wait()
    for copy in rows:
        copy.wait_send()


def polar_kernel(dev, col, gram, weight, mix, polar, projected, numer, inverse, code_gram):
    n_code, own, rank, tile_rows = dev.shape
    patients = own // VBLOCKS
    me_p, me_c = lax.axis_index("pat"), lax.axis_index("code")
    mine = [weight[me_p, pl.ds(me_c * patients + k, 1), :] for k in range(patients)]
    partials = [jnp.concatenate([gram[p, c] for p in range(gram.shape[0])], axis=0) for c in range(n_code)]
    sums = functools.reduce(jnp.add, partials)[:, :rank]
    code_gram[...] = sums
    weights = weight[...].reshape(-1, rank)
    inverse[...] = damped_inverse(sums * mm(weights, weights, 0, 0))
    products, iterates = [], []
    for k in range(patients):
        blocks = []
        for b in range(VBLOCKS):
            s = k * VBLOCKS + b
            value = None
            for c in range(n_code):
                term = dev[c, s].astype(f32) + partials[c][:, rank : rank + 1] * col[c, s : s + 1, :]
                value = term if value is None else value + term
            blocks.append(value)
        product = jnp.concatenate(blocks, axis=1)
        target = mm(mix[...] * mine[k], product)
        square = jnp.sum(jnp.sum(target * target, axis=1, keepdims=True), axis=0, keepdims=True)
        products.append(product)
        iterates.append(target / jnp.sqrt(square + epsilon))
    for step in range(NS_STEPS):
        grams = [mm(z, z, 1, 1) for z in iterates]
        iterates = [1.5 * z - 0.5 * mm(g, z) for g, z in zip(grams, iterates)]
    total = None
    for k in range(patients):
        polar[k] = iterates[k]
        value = mm(iterates[k], products[k], 1, 1)
        projected[k] = value
        term = value * mine[k]
        total = term if total is None else total + term
    numer[...] = total


def numer_kernel(n_pat, n_code, numer, result, pat_all, code_all, mid, send_p, recv_p, send_c, recv_c):
    me_p, me_c = lax.axis_index("pat"), lax.axis_index("code")
    greet(n_pat, n_code, me_p, me_c)
    copies = []
    for d in range(1, n_pat):
        copies.append(
            remote(numer, pat_all.at[me_p], send_p.at[d], recv_p.at[d], (lax.rem(me_p + d, n_pat), me_c))
        )
    pat_all[me_p] = numer[...]
    for copy in copies:
        copy.wait_recv()
    mid[...] = jnp.sum(pat_all[...], axis=0)
    more = []
    for d in range(1, n_code):
        more.append(
            remote(mid, code_all.at[me_c], send_c.at[d], recv_c.at[d], (me_p, lax.rem(me_c + d, n_code)))
        )
    code_all[me_c] = mid[...]
    for copy in more:
        copy.wait_recv()
    result[...] = jnp.sum(code_all[...], axis=0)
    for copy in copies + more:
        copy.wait_send()


def weight_kernel(numer, inverse, code_gram, polar, projected, mix_out, mix_gram, weight_out, spread):
    patients, rank, visits = polar.shape
    tile_rows = visits // VBLOCKS
    mix = mm(numer[...], inverse[...])
    mix_out[...] = mix
    square = mm(mix, mix, 0, 0)
    mix_gram[...] = square
    second = damped_inverse(square * code_gram[...])
    terms = jnp.concatenate(
        [jnp.sum(mix * projected[k], axis=0, keepdims=True) for k in range(patients)], axis=0
    )
    weight = jnp.maximum(mm(terms, second), 0.0)
    weight_out[...] = weight
    for k in range(patients):
        value = mm(mix * weight[k : k + 1, :], polar[k], 0, 0).astype(bf16)
        for b in range(VBLOCKS):
            spread[k * VBLOCKS + b] = value[:, b * tile_rows : (b + 1) * tile_rows]


def spread_kernel(
    n_pat, n_code, spread, weight, mix_gram, spread_all, inverse, weight_all, row, send_c, recv_c, send_p, recv_p, here
):
    me_p, me_c = lax.axis_index("pat"), lax.axis_index("code")
    greet(n_pat, n_code, me_p, me_c)
    first, bulk = [], []
    for d in range(1, n_code):
        where = (me_p, lax.rem(me_c + d, n_code))
        first.append(remote(weight, row.at[me_c], send_c.at[0, d], recv_c.at[0, d], where))
    for d in range(n_code - 1, 0, -1):
        where = (me_p, lax.rem(me_c + d, n_code))
        bulk.append(remote(spread, spread_all.at[me_c], send_c.at[1, d], recv_c.at[1, d], where))
    local = pltpu.make_async_copy(spread, spread_all.at[me_c], here.at[0])
    local.start()
    row[me_c] = weight[...]
    for copy in first:
        copy.wait_recv()
    second = []
    for d in range(1, n_pat):
        second.append(
            remote(row, weight_all.at[me_p], send_p.at[d], recv_p.at[d], (lax.rem(me_p + d, n_pat), me_c))
        )
    weight_all[me_p] = row[...]
    for copy in second:
        copy.wait_recv()
    rows = jnp.concatenate(
        [jnp.concatenate([weight_all[p, c] for c in range(n_code)], axis=0) for p in range(n_pat)], axis=0
    )
    inverse[...] = damped_inverse(mix_gram[...] * mm(rows, rows, 0, 0))
    for copy in bulk:
        copy.wait_recv()
    local.wait()
    for copy in first + second + bulk:
        copy.wait_send()


def code_kernel(list_ref, count_ref, visits_ref, tiles, spread, acc):
    slots, tile_rows, tile_cols = tiles.shape
    rank, codes = acc.shape
    acc[...] = jnp.zeros_like(acc)
    lane_at = lax.broadcasted_iota(jnp.int32, (rank, tile_rows), 1)
    for slot in range(slots):
        segment, code, limit = live_rows(list_ref, count_ref, visits_ref, slot, tile_rows)
        picked = jnp.where(lane_at < limit, spread[segment].astype(f32), 0.0).astype(bf16)
        where = pl.ds(pl.multiple_of(code * tile_cols, tile_cols), tile_cols)
        acc[:, where] += bmm(picked, tiles[slot])


def stacked_inverse(inverse):
    high = inverse.astype(bf16)
    low = (inverse - high.astype(f32)).astype(bf16)
    return jnp.concatenate([high, high, low], axis=1)


def solved_block(left, part):
    top = part.astype(bf16)
    rest = (part - top.astype(f32)).astype(bf16)
    return bmm(left, jnp.concatenate([top, rest, top], axis=0))


def solve_kernel(numer, inverse, result):
    codes = numer.shape[1]
    left = stacked_inverse(inverse[...])
    step = min(2048, codes)
    for start in range(0, codes, step):
        result[:, start : start + step] = solved_block(left, numer[:, start : start + step]).astype(bf16)


def quad_kernel(n_pat, numer, inverse, out, give, keep, pair, send_x, send_y, got_x, got_y, fin, sems, arrive):
    me_p, me_c = lax.axis_index("pat"), lax.axis_index("code")
    core, chip = lax.rem(me_p, 2), me_p // 2
    at_x, at_y = lax.rem(chip, 2), chip // 2
    width = numer.shape[1] // n_pat
    part = width // 2
    chips = [chip, at_y * 2 + 1 - at_x, (1 - at_y) * 2 + at_x, (1 - at_y) * 2 + 1 - at_x]
    partner = (chip * 2 + 1 - core, me_c)
    along_x, along_y = (chips[1] * 2 + core, me_c), (chips[2] * 2 + core, me_c)
    copies = []

    def lanes(index, half=None):
        if half is None:
            return pl.ds(pl.multiple_of(index * width, width), width)
        return pl.ds(pl.multiple_of(index * width + half * part, part), part)

    def go(src, dst, where):
        n = len(copies)
        copies.append(remote(src, dst, sems.at[n], arrive.at[n], where))
        return copies[-1]

    barrier = pltpu.get_barrier_semaphore()
    for where in (partner, along_x, along_y):
        pl.semaphore_signal(barrier, inc=1, device_id=where, device_id_type=MESH)
    pl.semaphore_wait(barrier, 3)

    left = stacked_inverse(inverse[...])
    order = (3, 1, 2, 0)
    pairs = {}
    for s in order:
        give[s] = solved_block(left, numer[:, lanes(chips[s] * 2 + 1 - core)]).astype(bf16)
        pairs[s] = go(give.at[s], pair.at[s], partner)
    for s in order:
        keep[s] = solved_block(left, numer[:, lanes(chips[s] * 2 + core)])
    for s in order:
        pairs[s].wait_recv()
        keep[s] += pair[s].astype(f32)
        if s == 3:
            send_x[0] = keep[3, :, :part].astype(bf16)
            x_far = go(send_x.at[0], got_x.at[0], along_x)
            send_y[0] = keep[3, :, part:].astype(bf16)
            y_far = go(send_y.at[0], got_y.at[0], along_y)
        elif s == 1:
            send_x[1] = keep[1, :, :part].astype(bf16)
            x_near = go(send_x.at[1], got_x.at[1], along_x)
        elif s == 2:
            send_y[1] = keep[2, :, part:].astype(bf16)
            y_near = go(send_y.at[1], got_y.at[1], along_y)
    x_far.wait_recv()
    send_y[2] = (keep[2, :, :part] + got_x[0].astype(f32)).astype(bf16)
    y_last = go(send_y.at[2], got_y.at[2], along_y)
    y_far.wait_recv()
    send_x[2] = (keep[1, :, part:] + got_y[0].astype(f32)).astype(bf16)
    x_last = go(send_x.at[2], got_x.at[2], along_x)
    x_near.wait_recv()
    y_last.wait_recv()
    low = keep[0, :, :part] + got_x[1].astype(f32) + got_y[2].astype(f32)
    fin[0] = jnp.maximum(low, 0.0).astype(bf16)
    spots = [out.at[:, lanes(me_p, h)] for h in range(2)]
    x_low = go(fin.at[0], spots[0], along_x)
    y_near.wait_recv()
    x_last.wait_recv()
    high = keep[0, :, part:] + got_y[1].astype(f32) + got_x[2].astype(f32)
    fin[1] = jnp.maximum(high, 0.0).astype(bf16)
    y_high = go(fin.at[1], spots[1], along_y)
    x_high = go(fin.at[1], spots[1], along_x)
    y_low = go(fin.at[0], spots[0], along_y)
    tail = [go(fin.at[0], spots[0], partner), go(fin.at[1], spots[1], partner)]
    out[:, lanes(me_p, 0)] = fin[0]
    out[:, lanes(me_p, 1)] = fin[1]

    def pass_on(s, half, where):
        spot = out.at[:, lanes(chips[s] * 2 + core, half)]
        return go(spot, spot, where)

    x_low.wait_recv()
    low_far = pass_on(1, 0, along_y)
    tail.append(pass_on(1, 0, partner))
    y_high.wait_recv()
    high_far = pass_on(2, 1, along_x)
    tail.append(pass_on(2, 1, partner))
    x_high.wait_recv()
    tail.append(pass_on(1, 1, partner))
    y_low.wait_recv()
    tail.append(pass_on(2, 0, partner))
    low_far.wait_recv()
    tail.append(pass_on(3, 0, partner))
    high_far.wait_recv()
    tail.append(pass_on(3, 1, partner))
    for copy in tail:
        copy.wait_recv()
    for copy in copies:
        copy.wait_send()


def reduce_kernel(n_pat, y, out, pair, half, got, send_a, recv_a, send_b, recv_b, send_c, recv_c, send_d, recv_d):
    me_p, me_c = lax.axis_index("pat"), lax.axis_index("code")
    chips = n_pat // 2
    chip, core = me_p // 2, lax.rem(me_p, 2)
    width = y.shape[1] // n_pat
    partner = (chip * 2 + 1 - core, me_c)

    def lanes(index):
        return pl.ds(pl.multiple_of(index * width, width), width)

    barrier = pltpu.get_barrier_semaphore()
    pl.semaphore_signal(barrier, inc=1, device_id=partner, device_id_type=MESH)
    for d in range(1, chips):
        pl.semaphore_signal(
            barrier, inc=1, device_id=(lax.rem(chip + d, chips) * 2 + core, me_c), device_id_type=MESH
        )
    pl.semaphore_wait(barrier, chips)

    order = list(range(1, chips)) + [0]
    stage_a, stage_b, stage_c, stage_d = [], [], [], []
    for d in order:
        q = lax.rem(chip + d, chips)
        stage_a.append(
            remote(y.at[:, lanes(q * 2 + 1 - core)], pair.at[d], send_a.at[d], recv_a.at[d], partner)
        )
    mine = None
    for n, d in enumerate(order):
        q = lax.rem(chip + d, chips)
        stage_a[n].wait_recv()
        value = y[:, lanes(q * 2 + core)].astype(f32) + pair[d].astype(f32)
        if d:
            half[d] = value.astype(bf16)
            stage_b.append(remote(half.at[d], got.at[d], send_b.at[d], recv_b.at[d], (q * 2 + core, me_c)))
        else:
            mine = value
    for copy in stage_b:
        copy.wait_recv()
    for d in range(1, chips):
        mine = mine + got[d].astype(f32)
    half[0] = jnp.maximum(mine, 0.0).astype(bf16)
    here = lanes(me_p)
    for d in range(1, chips):
        stage_c.append(
            remote(half.at[0], out.at[:, here], send_c.at[d], recv_c.at[d], (lax.rem(chip + d, chips) * 2 + core, me_c))
        )
    stage_d.append(remote(half.at[0], out.at[:, here], send_d.at[0], recv_d.at[0], partner))
    out[:, here] = half[0]
    for d in range(1, chips):
        stage_c[d - 1].wait_recv()
        q = lax.rem(chip + chips - d, chips)
        spot = out.at[:, lanes(q * 2 + core)]
        stage_d.append(remote(spot, spot, send_d.at[d], recv_d.at[d], partner))
    for copy in stage_d:
        copy.wait_recv()
    for copy in stage_a + stage_b + stage_c + stage_d:
        copy.wait_send()


def dma(*shape):
    return pltpu.SemaphoreType.DMA(shape)


def call(kernel, outs, n_in, scratch=(), smem=0, remote_id=None):
    if remote_id is None:
        params = pltpu.CompilerParams(vmem_limit_bytes=LIMIT)
    else:
        params = pltpu.CompilerParams(vmem_limit_bytes=LIMIT, collective_id=remote_id, has_side_effects=True)
    return pl.pallas_call(
        kernel,
        out_shape=[jax.ShapeDtypeStruct(s, d) for s, d in outs],
        in_specs=[SMEM] * smem + [VMEM] * (n_in - smem),
        out_specs=[VMEM] * len(outs),
        scratch_shapes=list(scratch),
        compiler_params=params,
    )


def body(tile_data, tile_list, tile_count, visit_counts, code_factor_t, visit_mix, patient_weight):
    n_pat, n_code = lax.axis_size("pat"), lax.axis_size("code")
    tiles = tile_data[0, 0]
    listing = jnp.transpose(tile_list[0], (1, 0, 2))
    count = tile_count[0]
    rank, codes = code_factor_t.shape
    slots, tile_rows, tile_cols = tiles.shape
    pat_row = visit_counts.shape[0]
    pat_own = pat_row // n_code
    segments, own = pat_row * VBLOCKS, pat_own * VBLOCKS
    chips = n_pat // 2
    width = codes // n_pat

    dev, col, gram = call(
        products_kernel,
        [((segments, rank, tile_rows), bf16), ((segments, tile_rows), f32), ((n_pat, rank // n_pat, 2 * rank), f32)],
        5,
        [pltpu.VMEM((2 * rank, codes), bf16), pltpu.VMEM((segments, rank, tile_rows), f32)],
        smem=3,
    )(listing, count, visit_counts, tiles, code_factor_t)
    dev_all, col_all, gram_all, weight_all = call(
        functools.partial(exchange_kernel, n_pat, n_code),
        [
            ((n_code, own, rank, tile_rows), bf16),
            ((n_code, own, tile_rows), f32),
            ((n_pat, n_code, rank // n_pat, 2 * rank), f32),
            ((n_pat, pat_row, rank), f32),
        ],
        4,
        [dma(3, n_code), dma(3, n_code), dma(2, n_pat), dma(2, n_pat), dma(4)],
        remote_id=1,
    )(dev, col, gram, patient_weight)
    square = ((rank, rank), f32)
    polar, projected, numer, inverse, code_gram = call(
        polar_kernel,
        [((pat_own, rank, VBLOCKS * tile_rows), f32), ((pat_own, rank, rank), f32), square, square, square],
        5,
    )(dev_all, col_all, gram_all, weight_all, visit_mix)
    (numer_sum,) = call(
        functools.partial(numer_kernel, n_pat, n_code),
        [square],
        1,
        [
            pltpu.VMEM((n_pat, rank, rank), f32),
            pltpu.VMEM((n_code, rank, rank), f32),
            pltpu.VMEM((rank, rank), f32),
            dma(n_pat),
            dma(n_pat),
            dma(n_code),
            dma(n_code),
        ],
        remote_id=2,
    )(numer)
    mix_new, mix_gram, weight_new, spread = call(
        weight_kernel, [square, square, ((pat_own, rank), f32), ((own, rank, tile_rows), bf16)], 5
    )(numer_sum, inverse, code_gram, polar, projected)
    spread_all, second = call(
        functools.partial(spread_kernel, n_pat, n_code),
        [((n_code, own, rank, tile_rows), bf16), square],
        3,
        [
            pltpu.VMEM((n_pat, n_code, pat_own, rank), f32),
            pltpu.VMEM((n_code, pat_own, rank), f32),
            dma(2, n_code),
            dma(2, n_code),
            dma(n_pat),
            dma(n_pat),
            dma(1),
        ],
        remote_id=3,
    )(spread, weight_new, mix_gram)
    (code_numer,) = call(code_kernel, [((rank, codes), f32)], 5, smem=3)(
        listing, count, visit_counts, tiles, spread_all.reshape(segments, rank, tile_rows)
    )
    if chips == 4:
        (code_new,) = call(
            functools.partial(quad_kernel, n_pat),
            [((rank, codes), bf16)],
            2,
            [
                pltpu.VMEM((chips, rank, width), bf16),
                pltpu.VMEM((chips, rank, width), f32),
                pltpu.VMEM((chips, rank, width), bf16),
                pltpu.VMEM((3, rank, width // 2), bf16),
                pltpu.VMEM((3, rank, width // 2), bf16),
                pltpu.VMEM((3, rank, width // 2), bf16),
                pltpu.VMEM((3, rank, width // 2), bf16),
                pltpu.VMEM((2, rank, width // 2), bf16),
                dma(24),
                dma(24),
            ],
            remote_id=4,
        )(code_numer, second)
    else:
        (solved,) = call(solve_kernel, [((rank, codes), bf16)], 2)(code_numer, second)
        (code_new,) = call(
            functools.partial(reduce_kernel, n_pat),
            [((rank, codes), bf16)],
            1,
            [pltpu.VMEM((chips, rank, width), bf16)] * 3 + [dma(chips)] * 8,
            remote_id=4,
        )(solved)
    return (code_new.astype(f32), mix_new, weight_new)


def solution(mesh):
    placed = (
        P("pat", "code", None, None, None),
        P("pat", "code", None, None),
        P("pat", "code"),
        P("pat"),
        P(None, "code"),
        P(),
        P("pat", None),
    )
    return jax.shard_map(
        body,
        mesh=mesh,
        in_specs=placed,
        out_specs=(P(None, "code"), P(), P(("pat", "code"), None)),
        check_vma=False,
    )
```

```python
import functools

import jax
import jax.numpy as jnp
from jax import lax
from jax.experimental import pallas as pl
from jax.experimental.pallas import tpu as pltpu
from jax.sharding import PartitionSpec as P

VBLOCKS = 2
NS_STEPS = 8
INVERSE_STEPS = 8
MESH = pl.DeviceIdType.MESH
damping = 0.1
epsilon = 1e-06

f32 = jnp.float32
bf16 = jnp.bfloat16
VMEM = pl.BlockSpec(memory_space=pltpu.VMEM)
SMEM = pl.BlockSpec(memory_space=pltpu.SMEM)
LIMIT = 32 * 1024 * 1024


def mm(left, right, left_dim=1, right_dim=0):
    return lax.dot_general(
        left,
        right,
        (((left_dim,), (right_dim,)), ((), ())),
        precision=lax.Precision.HIGHEST,
        preferred_element_type=f32,
    )


def bmm(left, right, left_dim=1, right_dim=0):
    return lax.dot_general(
        left, right, (((left_dim,), (right_dim,)), ((), ())), preferred_element_type=f32
    )


def damped_inverse(gram):
    size = gram.shape[0]
    row_at = lax.broadcasted_iota(jnp.int32, (size, size), 0)
    lane_at = lax.broadcasted_iota(jnp.int32, (size, size), 1)
    eye = jnp.where(row_at == lane_at, 1.0, 0.0)
    trace = jnp.sum(jnp.sum(gram * eye, axis=1, keepdims=True), axis=0, keepdims=True)
    mean = trace * (1.0 / size)
    unscale = 1.0 / (mean * (0.5 * size + damping))
    a = gram * unscale + eye * (damping / (0.5 * size + damping))
    rest = eye - a
    tau = (size + 2.0 * damping) / size
    x = eye
    for step in range(INVERSE_STEPS):
        twice = 2.0 * tau * tau
        gain = twice / (twice - 1.0)
        if step == 0:
            x, square = x + rest, mm(rest, rest)
        else:
            both = mm(rest, jnp.concatenate([x, rest], axis=1))
            x, square = x + both[:, :size], both[:, size:]
        x = x * gain
        rest = square * gain - eye * (1.0 / (twice - 1.0))
        tau = twice - 1.0
    x = x + mm(x, eye - mm(a, x))
    return x * unscale


def live_rows(list_ref, count_ref, visits_ref, slot, tile_rows):
    owner, block, code = list_ref[0, 0, slot], list_ref[1, 0, slot], list_ref[2, 0, slot]
    limit = jnp.where(slot < count_ref[0], visits_ref[owner] - block * tile_rows, 0)
    return owner * VBLOCKS + block, code, limit


def products_kernel(list_ref, count_ref, visits_ref, tiles, factor, dev, col, gram, split, acc):
    slots, tile_rows, tile_cols = tiles.shape
    rank, codes = factor.shape
    step = min(2048, codes)
    total = jnp.zeros((2 * rank, 2 * rank), f32)
    profile = jnp.zeros((rank, 1), f32)
    for start in range(0, codes, step):
        part = factor[:, start : start + step]
        high = part.astype(bf16)
        split[:rank, start : start + step] = high
        split[rank:, start : start + step] = (part - high.astype(f32)).astype(bf16)
        profile += jnp.sum(part, axis=1, keepdims=True)
        both = split[:, start : start + step]
        total += bmm(both, both, 1, 1)
    profile = profile * (1.0 / codes)
    square = total[:rank, :rank] + total[:rank, rank:] + total[rank:, :rank] + total[rank:, rank:]
    both = jnp.concatenate([square, jnp.broadcast_to(profile, (rank, rank))], axis=1)
    rows = gram.shape[1]
    for p in range(gram.shape[0]):
        gram[p] = both[p * rows : (p + 1) * rows, :]
    acc[...] = jnp.zeros_like(acc)
    lane_at = lax.broadcasted_iota(jnp.int32, (rank, tile_rows), 1)
    for slot in range(slots):
        segment, code, limit = live_rows(list_ref, count_ref, visits_ref, slot, tile_rows)
        picked = split[:rank, pl.ds(pl.multiple_of(code * tile_cols, tile_cols), tile_cols)]
        contrib = bmm(picked, tiles[slot], 1, 1)
        acc[segment] += jnp.where(lane_at < limit, contrib, 0.0)
    whole = 1.0 / jnp.sum(profile, axis=0, keepdims=True)
    for segment in range(acc.shape[0]):
        value = acc[segment]
        column = jnp.sum(value, axis=0, keepdims=True) * whole
        col[segment : segment + 1, :] = column
        dev[segment] = (value - profile * column).astype(bf16)


def code_peer(me, distance, n_code):
    return lax.rem(me + distance, n_code)


def greet(n_pat, n_code, me_p, me_c):
    barrier = pltpu.get_barrier_semaphore()
    for d in range(1, n_code):
        pl.semaphore_signal(barrier, inc=1, device_id=(me_p, lax.rem(me_c + d, n_code)), device_id_type=MESH)
    for d in range(1, n_pat):
        pl.semaphore_signal(barrier, inc=1, device_id=(lax.rem(me_p + d, n_pat), me_c), device_id_type=MESH)
    pl.semaphore_wait(barrier, n_code + n_pat - 2)


def remote(src, dst, send, recv, where):
    copy = pltpu.make_async_remote_copy(
        src_ref=src, dst_ref=dst, send_sem=send, recv_sem=recv, device_id=where, device_id_type=MESH
    )
    copy.start()
    return copy


def polar_factors(products, mix, mine):
    rank = mix.shape[0]
    row_at = lax.broadcasted_iota(jnp.int32, (rank, rank), 0)
    lane_at = lax.broadcasted_iota(jnp.int32, (rank, rank), 1)
    eye = jnp.where(row_at == lane_at, 1.0, 0.0)
    targets = [mm(mix * w, x) for w, x in zip(mine, products)]
    crosses, grams, scales = [], [], []
    for target, product in zip(targets, products):
        both = mm(target, jnp.concatenate([target, product], axis=0), 1, 1)
        gram = both[:, :rank]
        norm = jnp.sum(jnp.sum(gram * eye, axis=1, keepdims=True), axis=0, keepdims=True) + epsilon
        crosses.append(both[:, rank:])
        grams.append(gram / norm)
        scales.append(1.0 / jnp.sqrt(norm))
    maps = None
    for step in range(NS_STEPS):
        steps = [1.5 * eye - 0.5 * g for g in grams]
        if step == 0:
            maps, halves = steps, [mm(p, g) for p, g in zip(steps, grams)]
        elif step < NS_STEPS - 1:
            wide = [mm(p, jnp.concatenate([g, q], axis=1)) for p, g, q in zip(steps, grams, maps)]
            halves, maps = [w[:, :rank] for w in wide], [w[:, rank:] for w in wide]
        else:
            maps = [mm(p, q) for p, q in zip(steps, maps)]
        if step < NS_STEPS - 1:
            grams = [mm(h, p) for h, p in zip(halves, steps)]
    maps = [q * scale for q, scale in zip(maps, scales)]
    polars = [mm(q, target) for q, target in zip(maps, targets)]
    return polars, [mm(q, cross) for q, cross in zip(maps, crosses)]


def core_kernel(
    n_pat,
    n_code,
    dev,
    col,
    gram,
    weight,
    mix_in,
    spread,
    inverse,
    mix_out,
    weight_out,
    dev_all,
    col_all,
    gram_all,
    old_all,
    numer_c,
    numer_p,
    mid,
    polar_all,
    row,
    weight_all,
    send_c,
    recv_c,
    send_p,
    recv_p,
):
    me_p, me_c = lax.axis_index("pat"), lax.axis_index("code")
    segments, rank, tile_rows = dev.shape
    own = segments // n_code
    patients = own // VBLOCKS
    half = rank // 2

    def to_code(kind, src, dst):
        copies = []
        for d in range(n_code - 1, 0, -1):
            where = (me_p, lax.rem(me_c + d, n_code))
            copies.append(remote(src(d), dst, send_c.at[kind, d], recv_c.at[kind, d], where))
        return copies

    def to_pat(kind, src, dst):
        copies = []
        for d in range(1, n_pat):
            where = (lax.rem(me_p + d, n_pat), me_c)
            copies.append(remote(src, dst, send_p.at[kind, d], recv_p.at[kind, d], where))
        return copies

    def share(d):
        return pl.ds(lax.rem(me_c + d, n_code) * own, own)

    greet(n_pat, n_code, me_p, me_c)
    gram_c = to_code(0, lambda d: gram.at[me_p], gram_all.at[me_p, me_c])
    col_c = to_code(1, lambda d: col.at[share(d)], col_all.at[me_c])
    dev_c = to_code(2, lambda d: dev.at[share(d)], dev_all.at[me_c])
    old_p = to_pat(0, weight, old_all.at[me_p])
    gram_all[me_p, me_c] = gram[me_p]
    old_all[me_p] = weight[...]
    col_all[me_c] = col[share(0)]
    dev_all[me_c] = dev[share(0)]
    for copy in gram_c:
        copy.wait_recv()
    gram_p = to_pat(1, gram_all.at[me_p], gram_all.at[me_p])
    for copy in old_p + gram_p:
        copy.wait_recv()
    partials = [jnp.concatenate([gram_all[p, c] for p in range(n_pat)], axis=0) for c in range(n_code)]
    code_gram = functools.reduce(jnp.add, partials)[:, :rank]
    olds = old_all[...].reshape(-1, rank)
    first = damped_inverse(code_gram * mm(olds, olds, 0, 0))
    mine = [weight[pl.ds(me_c * patients + k, 1), :] for k in range(patients)]

    for copy in col_c + dev_c:
        copy.wait_recv()
    products = []
    for k in range(patients):
        blocks = []
        for b in range(VBLOCKS):
            s = k * VBLOCKS + b
            value = None
            for c in range(n_code):
                term = dev_all[c, s].astype(f32) + partials[c][:, rank : rank + 1] * col_all[c, s : s + 1, :]
                value = term if value is None else value + term
            blocks.append(value)
        products.append(jnp.concatenate(blocks, axis=1))
    polars, projected = polar_factors(products, mix_in[...], mine)
    total = functools.reduce(jnp.add, [p * w for p, w in zip(projected, mine)])
    numer_c[me_c] = jnp.concatenate([total[:half], total[half:]], axis=1)
    numer_z = to_code(3, lambda d: numer_c.at[me_c], numer_c.at[me_c])
    for k in range(patients):
        for b in range(VBLOCKS):
            piece = polars[k][:, b * tile_rows : (b + 1) * tile_rows]
            polar_all[me_c, k * VBLOCKS + b] = piece.astype(bf16)
    polar_c = to_code(4, lambda d: polar_all.at[me_c], polar_all.at[me_c])
    for copy in numer_z:
        copy.wait_recv()
    mid[...] = jnp.sum(numer_c[...], axis=0)
    numer_x = to_pat(2, mid, numer_p.at[me_p])
    numer_p[me_p] = mid[...]
    for copy in numer_x:
        copy.wait_recv()
    packed = jnp.sum(numer_p[...], axis=0)
    numer = jnp.concatenate([packed[:, :rank], packed[:, rank:]], axis=0)

    mix = mm(numer, first)
    mix_out[...] = mix
    square = mm(mix, mix, 0, 0)
    terms = jnp.concatenate([jnp.sum(mix * projected[k], axis=0, keepdims=True) for k in range(patients)], axis=0)
    fresh = jnp.maximum(mm(terms, damped_inverse(square * code_gram)), 0.0)
    weight_out[...] = fresh
    row[me_c] = fresh
    row_c = to_code(5, lambda d: row.at[me_c], row.at[me_c])
    for copy in row_c:
        copy.wait_recv()
    row_p = to_pat(3, row, weight_all.at[me_p])
    weight_all[me_p] = row[...]
    for copy in polar_c:
        copy.wait_recv()
    for c in range(n_code):
        for k in range(patients):
            scaled = mix * row[c, k : k + 1, :]
            high = scaled.astype(bf16)
            left = jnp.concatenate([high, (scaled - high.astype(f32)).astype(bf16)], axis=0)
            for b in range(VBLOCKS):
                s = k * VBLOCKS + b
                part = polar_all[c, s]
                spread[c * own + s] = bmm(left, jnp.concatenate([part, part], axis=0), 0, 0).astype(bf16)
    for copy in row_p:
        copy.wait_recv()
    rows = jnp.concatenate(
        [jnp.concatenate([weight_all[p, c] for c in range(n_code)], axis=0) for p in range(n_pat)], axis=0
    )
    inverse[...] = damped_inverse(square * mm(rows, rows, 0, 0))
    for copy in gram_c + col_c + dev_c + old_p + gram_p + numer_z + polar_c + numer_x + row_c + row_p:
        copy.wait_send()


def code_kernel(list_ref, count_ref, visits_ref, tiles, spread, mix, weight, acc, mix_out, weight_out):
    mix_out[...] = mix[...]
    weight_out[...] = weight[...]
    slots, tile_rows, tile_cols = tiles.shape
    rank, codes = acc.shape
    acc[...] = jnp.zeros_like(acc)
    lane_at = lax.broadcasted_iota(jnp.int32, (rank, tile_rows), 1)
    for slot in range(slots):
        segment, code, limit = live_rows(list_ref, count_ref, visits_ref, slot, tile_rows)
        picked = jnp.where(lane_at < limit, spread[segment].astype(f32), 0.0).astype(bf16)
        where = pl.ds(pl.multiple_of(code * tile_cols, tile_cols), tile_cols)
        acc[:, where] += bmm(picked, tiles[slot])


def stacked_inverse(inverse):
    high = inverse.astype(bf16)
    low = (inverse - high.astype(f32)).astype(bf16)
    return jnp.concatenate([high, high, low], axis=1)


def solved_block(left, part):
    top = part.astype(bf16)
    rest = (part - top.astype(f32)).astype(bf16)
    return bmm(left, jnp.concatenate([top, rest, top], axis=0))


def solve_kernel(numer, inverse, result):
    codes = numer.shape[1]
    left = stacked_inverse(inverse[...])
    step = min(2048, codes)
    for start in range(0, codes, step):
        result[:, start : start + step] = solved_block(left, numer[:, start : start + step]).astype(bf16)


def quad_kernel(n_pat, numer, inverse, out, give, keep, pair, send_x, send_y, got_x, got_y, fin, sems, arrive):
    me_p, me_c = lax.axis_index("pat"), lax.axis_index("code")
    core, chip = lax.rem(me_p, 2), me_p // 2
    at_x, at_y = lax.rem(chip, 2), chip // 2
    width = numer.shape[1] // n_pat
    part = width // 2
    chips = [chip, at_y * 2 + 1 - at_x, (1 - at_y) * 2 + at_x, (1 - at_y) * 2 + 1 - at_x]
    partner = (chip * 2 + 1 - core, me_c)
    along_x, along_y = (chips[1] * 2 + core, me_c), (chips[2] * 2 + core, me_c)
    copies = []

    def lanes(index, half=None):
        if half is None:
            return pl.ds(pl.multiple_of(index * width, width), width)
        return pl.ds(pl.multiple_of(index * width + half * part, part), part)

    def go(src, dst, where):
        n = len(copies)
        copies.append(remote(src, dst, sems.at[n], arrive.at[n], where))
        return copies[-1]

    barrier = pltpu.get_barrier_semaphore()
    for where in (partner, along_x, along_y):
        pl.semaphore_signal(barrier, inc=1, device_id=where, device_id_type=MESH)
    pl.semaphore_wait(barrier, 3)

    left = stacked_inverse(inverse[...])
    order = (3, 1, 2, 0)
    pairs = {}
    for s in order:
        give[s] = solved_block(left, numer[:, lanes(chips[s] * 2 + 1 - core)]).astype(bf16)
        pairs[s] = go(give.at[s], pair.at[s], partner)
    for s in order:
        keep[s] = solved_block(left, numer[:, lanes(chips[s] * 2 + core)])
    for s in order:
        pairs[s].wait_recv()
        keep[s] += pair[s].astype(f32)
        if s == 3:
            send_x[0] = keep[3, :, :part].astype(bf16)
            x_far = go(send_x.at[0], got_x.at[0], along_x)
            send_y[0] = keep[3, :, part:].astype(bf16)
            y_far = go(send_y.at[0], got_y.at[0], along_y)
        elif s == 1:
            send_x[1] = keep[1, :, :part].astype(bf16)
            x_near = go(send_x.at[1], got_x.at[1], along_x)
        elif s == 2:
            send_y[1] = keep[2, :, part:].astype(bf16)
            y_near = go(send_y.at[1], got_y.at[1], along_y)
    x_far.wait_recv()
    send_y[2] = (keep[2, :, :part] + got_x[0].astype(f32)).astype(bf16)
    y_last = go(send_y.at[2], got_y.at[2], along_y)
    y_far.wait_recv()
    send_x[2] = (keep[1, :, part:] + got_y[0].astype(f32)).astype(bf16)
    x_last = go(send_x.at[2], got_x.at[2], along_x)
    x_near.wait_recv()
    y_last.wait_recv()
    low = keep[0, :, :part] + got_x[1].astype(f32) + got_y[2].astype(f32)
    fin[0] = jnp.maximum(low, 0.0).astype(bf16)
    spots = [out.at[:, lanes(me_p, h)] for h in range(2)]
    x_low = go(fin.at[0], spots[0], along_x)
    y_near.wait_recv()
    x_last.wait_recv()
    high = keep[0, :, part:] + got_y[1].astype(f32) + got_x[2].astype(f32)
    fin[1] = jnp.maximum(high, 0.0).astype(bf16)
    y_high = go(fin.at[1], spots[1], along_y)
    x_high = go(fin.at[1], spots[1], along_x)
    y_low = go(fin.at[0], spots[0], along_y)
    tail = [go(fin.at[0], spots[0], partner), go(fin.at[1], spots[1], partner)]
    out[:, lanes(me_p, 0)] = fin[0]
    out[:, lanes(me_p, 1)] = fin[1]

    def pass_on(s, half, where):
        spot = out.at[:, lanes(chips[s] * 2 + core, half)]
        return go(spot, spot, where)

    x_low.wait_recv()
    low_far = pass_on(1, 0, along_y)
    tail.append(pass_on(1, 0, partner))
    y_high.wait_recv()
    high_far = pass_on(2, 1, along_x)
    tail.append(pass_on(2, 1, partner))
    x_high.wait_recv()
    tail.append(pass_on(1, 1, partner))
    y_low.wait_recv()
    tail.append(pass_on(2, 0, partner))
    low_far.wait_recv()
    tail.append(pass_on(3, 0, partner))
    high_far.wait_recv()
    tail.append(pass_on(3, 1, partner))
    for copy in tail:
        copy.wait_recv()
    for copy in copies:
        copy.wait_send()


def reduce_kernel(n_pat, y, out, pair, half, got, send_a, recv_a, send_b, recv_b, send_c, recv_c, send_d, recv_d):
    me_p, me_c = lax.axis_index("pat"), lax.axis_index("code")
    chips = n_pat // 2
    chip, core = me_p // 2, lax.rem(me_p, 2)
    width = y.shape[1] // n_pat
    partner = (chip * 2 + 1 - core, me_c)

    def lanes(index):
        return pl.ds(pl.multiple_of(index * width, width), width)

    barrier = pltpu.get_barrier_semaphore()
    pl.semaphore_signal(barrier, inc=1, device_id=partner, device_id_type=MESH)
    for d in range(1, chips):
        pl.semaphore_signal(
            barrier, inc=1, device_id=(lax.rem(chip + d, chips) * 2 + core, me_c), device_id_type=MESH
        )
    pl.semaphore_wait(barrier, chips)

    order = list(range(1, chips)) + [0]
    stage_a, stage_b, stage_c, stage_d = [], [], [], []
    for d in order:
        q = lax.rem(chip + d, chips)
        stage_a.append(
            remote(y.at[:, lanes(q * 2 + 1 - core)], pair.at[d], send_a.at[d], recv_a.at[d], partner)
        )
    mine = None
    for n, d in enumerate(order):
        q = lax.rem(chip + d, chips)
        stage_a[n].wait_recv()
        value = y[:, lanes(q * 2 + core)].astype(f32) + pair[d].astype(f32)
        if d:
            half[d] = value.astype(bf16)
            stage_b.append(remote(half.at[d], got.at[d], send_b.at[d], recv_b.at[d], (q * 2 + core, me_c)))
        else:
            mine = value
    for copy in stage_b:
        copy.wait_recv()
    for d in range(1, chips):
        mine = mine + got[d].astype(f32)
    half[0] = jnp.maximum(mine, 0.0).astype(bf16)
    here = lanes(me_p)
    for d in range(1, chips):
        stage_c.append(
            remote(half.at[0], out.at[:, here], send_c.at[d], recv_c.at[d], (lax.rem(chip + d, chips) * 2 + core, me_c))
        )
    stage_d.append(remote(half.at[0], out.at[:, here], send_d.at[0], recv_d.at[0], partner))
    out[:, here] = half[0]
    for d in range(1, chips):
        stage_c[d - 1].wait_recv()
        q = lax.rem(chip + chips - d, chips)
        spot = out.at[:, lanes(q * 2 + core)]
        stage_d.append(remote(spot, spot, send_d.at[d], recv_d.at[d], partner))
    for copy in stage_d:
        copy.wait_recv()
    for copy in stage_a + stage_b + stage_c + stage_d:
        copy.wait_send()


def dma(*shape):
    return pltpu.SemaphoreType.DMA(shape)


def call(kernel, outs, n_in, scratch=(), smem=0, remote_id=None):
    if remote_id is None:
        params = pltpu.CompilerParams(vmem_limit_bytes=LIMIT)
    else:
        params = pltpu.CompilerParams(vmem_limit_bytes=LIMIT, collective_id=remote_id, has_side_effects=True)
    return pl.pallas_call(
        kernel,
        out_shape=[jax.ShapeDtypeStruct(s, d) for s, d in outs],
        in_specs=[SMEM] * smem + [VMEM] * (n_in - smem),
        out_specs=[VMEM] * len(outs),
        scratch_shapes=list(scratch),
        compiler_params=params,
    )


def body(tile_data, tile_list, tile_count, visit_counts, code_factor_t, visit_mix, patient_weight):
    n_pat, n_code = lax.axis_size("pat"), lax.axis_size("code")
    tiles = tile_data[0, 0]
    listing = jnp.transpose(tile_list[0], (1, 0, 2))
    count = tile_count[0]
    rank, codes = code_factor_t.shape
    slots, tile_rows, tile_cols = tiles.shape
    pat_row = visit_counts.shape[0]
    pat_own = pat_row // n_code
    segments, own = pat_row * VBLOCKS, pat_own * VBLOCKS
    chips = n_pat // 2
    width = codes // n_pat

    dev, col, gram = call(
        products_kernel,
        [((segments, rank, tile_rows), bf16), ((segments, tile_rows), f32), ((n_pat, rank // n_pat, 2 * rank), f32)],
        5,
        [pltpu.VMEM((2 * rank, codes), bf16), pltpu.VMEM((segments, rank, tile_rows), f32)],
        smem=3,
    )(listing, count, visit_counts, tiles, code_factor_t)
    square = ((rank, rank), f32)
    fresh = ((pat_own, rank), f32)
    spread, second, mix_kept, weight_kept = call(
        functools.partial(core_kernel, n_pat, n_code),
        [((segments, rank, tile_rows), bf16), square, square, fresh],
        5,
        [
            pltpu.VMEM((n_code, own, rank, tile_rows), bf16),
            pltpu.VMEM((n_code, own, tile_rows), f32),
            pltpu.VMEM((n_pat, n_code, rank // n_pat, 2 * rank), f32),
            pltpu.VMEM((n_pat, pat_row, rank), f32),
            pltpu.VMEM((n_code, rank // 2, 2 * rank), f32),
            pltpu.VMEM((n_pat, rank // 2, 2 * rank), f32),
            pltpu.VMEM((rank // 2, 2 * rank), f32),
            pltpu.VMEM((n_code, own, rank, tile_rows), bf16),
            pltpu.VMEM((n_code, pat_own, rank), f32),
            pltpu.VMEM((n_pat, n_code, pat_own, rank), f32),
            dma(6, n_code),
            dma(6, n_code),
            dma(4, n_pat),
            dma(4, n_pat),
        ],
        remote_id=1,
    )(dev, col, gram, patient_weight, visit_mix)
    code_numer, mix_new, weight_new = call(code_kernel, [((rank, codes), f32), square, fresh], 7, smem=3)(
        listing, count, visit_counts, tiles, spread, mix_kept, weight_kept
    )
    if chips == 4:
        (code_new,) = call(
            functools.partial(quad_kernel, n_pat),
            [((rank, codes), bf16)],
            2,
            [
                pltpu.VMEM((chips, rank, width), bf16),
                pltpu.VMEM((chips, rank, width), f32),
                pltpu.VMEM((chips, rank, width), bf16),
                pltpu.VMEM((3, rank, width // 2), bf16),
                pltpu.VMEM((3, rank, width // 2), bf16),
                pltpu.VMEM((3, rank, width // 2), bf16),
                pltpu.VMEM((3, rank, width // 2), bf16),
                pltpu.VMEM((2, rank, width // 2), bf16),
                dma(24),
                dma(24),
            ],
            remote_id=4,
        )(code_numer, second)
    else:
        (solved,) = call(solve_kernel, [((rank, codes), bf16)], 2)(code_numer, second)
        (code_new,) = call(
            functools.partial(reduce_kernel, n_pat),
            [((rank, codes), bf16)],
            1,
            [pltpu.VMEM((chips, rank, width), bf16)] * 3 + [dma(chips)] * 8,
            remote_id=4,
        )(solved)
    return (code_new.astype(f32), mix_new, weight_new)


def solution(mesh):
    placed = (
        P("pat", "code", None, None, None),
        P("pat", "code", None, None),
        P("pat", "code"),
        P("pat"),
        P(None, "code"),
        P(),
        P("pat", None),
    )
    return jax.shard_map(
        body,
        mesh=mesh,
        in_specs=placed,
        out_specs=(P(None, "code"), P(), P(("pat", "code"), None)),
        check_vma=False,
    )
```

```python
import functools

import jax
import jax.numpy as jnp
from jax import lax
from jax.experimental import pallas as pl
from jax.experimental.pallas import tpu as pltpu
from jax.sharding import PartitionSpec as P

VBLOCKS = 2
NS_STEPS = 8
INVERSE_STEPS = 7
STREAMS = 2
MESH = pl.DeviceIdType.MESH
damping = 0.1
epsilon = 1e-06

f32 = jnp.float32
bf16 = jnp.bfloat16
VMEM = pl.BlockSpec(memory_space=pltpu.VMEM)
SMEM = pl.BlockSpec(memory_space=pltpu.SMEM)
LIMIT = 32 * 1024 * 1024


def mm(left, right, left_dim=1, right_dim=0):
    return lax.dot_general(
        left,
        right,
        (((left_dim,), (right_dim,)), ((), ())),
        precision=lax.Precision.HIGHEST,
        preferred_element_type=f32,
    )


def bmm(left, right, left_dim=1, right_dim=0):
    return lax.dot_general(
        left, right, (((left_dim,), (right_dim,)), ((), ())), preferred_element_type=f32
    )


def damped_inverse(gram):
    size = gram.shape[0]
    row_at = lax.broadcasted_iota(jnp.int32, (size, size), 0)
    lane_at = lax.broadcasted_iota(jnp.int32, (size, size), 1)
    eye = jnp.where(row_at == lane_at, 1.0, 0.0)
    trace = jnp.sum(jnp.sum(gram * eye, axis=1, keepdims=True), axis=0, keepdims=True)
    mean = trace * (1.0 / size)
    unscale = 1.0 / (mean * (0.5 * size + damping))
    a = gram * unscale + eye * (damping / (0.5 * size + damping))
    rest = eye - a
    tau = (size + 2.0 * damping) / size
    x = eye
    for step in range(INVERSE_STEPS):
        twice = 2.0 * tau * tau
        gain = twice / (twice - 1.0)
        if step == 0:
            x, square = x + rest, mm(rest, rest)
        else:
            both = mm(rest, jnp.concatenate([x, rest], axis=1))
            x, square = x + both[:, :size], both[:, size:]
        x = x * gain
        rest = square * gain - eye * (1.0 / (twice - 1.0))
        tau = twice - 1.0
    x = x + mm(x, eye - mm(a, x))
    return x * unscale


def live_rows(list_ref, count_ref, visits_ref, slot, tile_rows):
    owner, block, code = list_ref[0, 0, slot], list_ref[1, 0, slot], list_ref[2, 0, slot]
    limit = jnp.where(slot < count_ref[0], visits_ref[owner] - block * tile_rows, 0)
    return owner * VBLOCKS + block, code, limit


def products_kernel(list_ref, count_ref, visits_ref, tiles, factor, dev, col, gram, split, acc):
    slots, tile_rows, tile_cols = tiles.shape
    rank, codes = factor.shape
    step = min(2048, codes)
    total = jnp.zeros((2 * rank, 2 * rank), f32)
    profile = jnp.zeros((rank, 1), f32)
    for start in range(0, codes, step):
        part = factor[:, start : start + step]
        high = part.astype(bf16)
        split[:rank, start : start + step] = high
        split[rank:, start : start + step] = (part - high.astype(f32)).astype(bf16)
        profile += jnp.sum(part, axis=1, keepdims=True)
        both = split[:, start : start + step]
        total += bmm(both, both, 1, 1)
    profile = profile * (1.0 / codes)
    square = total[:rank, :rank] + total[:rank, rank:] + total[rank:, :rank] + total[rank:, rank:]
    both = jnp.concatenate([square, jnp.broadcast_to(profile, (rank, rank))], axis=1)
    rows = gram.shape[1]
    for p in range(gram.shape[0]):
        gram[p] = both[p * rows : (p + 1) * rows, :]
    acc[...] = jnp.zeros_like(acc)
    lane_at = lax.broadcasted_iota(jnp.int32, (rank, tile_rows), 1)
    for slot in range(slots):
        segment, code, limit = live_rows(list_ref, count_ref, visits_ref, slot, tile_rows)
        picked = split[:rank, pl.ds(pl.multiple_of(code * tile_cols, tile_cols), tile_cols)]
        contrib = bmm(picked, tiles[slot], 1, 1)
        acc[segment] += jnp.where(lane_at < limit, contrib, 0.0)
    whole = 1.0 / jnp.sum(profile, axis=0, keepdims=True)
    for segment in range(acc.shape[0]):
        value = acc[segment]
        column = jnp.sum(value, axis=0, keepdims=True) * whole
        col[segment : segment + 1, :] = column
        dev[segment] = (value - profile * column).astype(bf16)


def code_peer(me, distance, n_code):
    return lax.rem(me + distance, n_code)


def greet(n_pat, n_code, me_p, me_c):
    barrier = pltpu.get_barrier_semaphore()
    for d in range(1, n_code):
        pl.semaphore_signal(barrier, inc=1, device_id=(me_p, lax.rem(me_c + d, n_code)), device_id_type=MESH)
    for d in range(1, n_pat):
        pl.semaphore_signal(barrier, inc=1, device_id=(lax.rem(me_p + d, n_pat), me_c), device_id_type=MESH)
    pl.semaphore_wait(barrier, n_code + n_pat - 2)


def remote(src, dst, send, recv, where):
    copy = pltpu.make_async_remote_copy(
        src_ref=src, dst_ref=dst, send_sem=send, recv_sem=recv, device_id=where, device_id_type=MESH
    )
    copy.start()
    return copy


def polar_factors(products, mix, mine):
    rank = mix.shape[0]
    row_at = lax.broadcasted_iota(jnp.int32, (rank, rank), 0)
    lane_at = lax.broadcasted_iota(jnp.int32, (rank, rank), 1)
    eye = jnp.where(row_at == lane_at, 1.0, 0.0)
    targets = [mm(mix * w, x) for w, x in zip(mine, products)]
    crosses, grams, scales = [], [], []
    for target, product in zip(targets, products):
        both = mm(target, jnp.concatenate([target, product], axis=0), 1, 1)
        gram = both[:, :rank]
        norm = jnp.sum(jnp.sum(gram * eye, axis=1, keepdims=True), axis=0, keepdims=True) + epsilon
        crosses.append(both[:, rank:])
        grams.append(gram / norm)
        scales.append(1.0 / jnp.sqrt(norm))
    maps = None
    for step in range(NS_STEPS):
        steps = [1.5 * eye - 0.5 * g for g in grams]
        if step == 0:
            maps, halves = steps, [mm(p, g) for p, g in zip(steps, grams)]
        elif step < NS_STEPS - 1:
            wide = [mm(p, jnp.concatenate([g, q], axis=1)) for p, g, q in zip(steps, grams, maps)]
            halves, maps = [w[:, :rank] for w in wide], [w[:, rank:] for w in wide]
        else:
            maps = [mm(p, q) for p, q in zip(steps, maps)]
        if step < NS_STEPS - 1:
            grams = [mm(h, p) for h, p in zip(halves, steps)]
    maps = [q * scale for q, scale in zip(maps, scales)]
    polars = [mm(q, target) for q, target in zip(maps, targets)]
    return polars, [mm(q, cross) for q, cross in zip(maps, crosses)]


def core_kernel(
    n_pat,
    n_code,
    dev,
    col,
    gram,
    weight,
    mix_in,
    spread,
    inverse,
    mix_out,
    weight_out,
    dev_all,
    col_all,
    gram_all,
    old_all,
    numer_c,
    numer_p,
    mid,
    polar_all,
    row,
    weight_all,
    send_c,
    recv_c,
    send_p,
    recv_p,
):
    me_p, me_c = lax.axis_index("pat"), lax.axis_index("code")
    segments, rank, tile_rows = dev.shape
    own = segments // n_code
    patients = own // VBLOCKS
    half = rank // 2

    def to_code(kind, src, dst):
        copies = []
        for d in range(n_code - 1, 0, -1):
            where = (me_p, lax.rem(me_c + d, n_code))
            copies.append(remote(src(d), dst, send_c.at[kind, d], recv_c.at[kind, d], where))
        return copies

    def to_pat(kind, src, dst):
        copies = []
        for d in range(1, n_pat):
            where = (lax.rem(me_p + d, n_pat), me_c)
            copies.append(remote(src, dst, send_p.at[kind, d], recv_p.at[kind, d], where))
        return copies

    def share(d):
        return pl.ds(lax.rem(me_c + d, n_code) * own, own)

    greet(n_pat, n_code, me_p, me_c)
    gram_c = to_code(0, lambda d: gram.at[me_p], gram_all.at[me_p, me_c])
    col_c = to_code(1, lambda d: col.at[share(d)], col_all.at[me_c])
    dev_c = to_code(2, lambda d: dev.at[share(d)], dev_all.at[me_c])
    old_p = to_pat(0, weight, old_all.at[me_p])
    gram_all[me_p, me_c] = gram[me_p]
    old_all[me_p] = weight[...]
    col_all[me_c] = col[share(0)]
    dev_all[me_c] = dev[share(0)]
    for copy in gram_c:
        copy.wait_recv()
    gram_p = to_pat(1, gram_all.at[me_p], gram_all.at[me_p])
    for copy in old_p + gram_p:
        copy.wait_recv()
    partials = [jnp.concatenate([gram_all[p, c] for p in range(n_pat)], axis=0) for c in range(n_code)]
    code_gram = functools.reduce(jnp.add, partials)[:, :rank]
    olds = old_all[...].reshape(-1, rank)
    first = damped_inverse(code_gram * mm(olds, olds, 0, 0))
    mine = [weight[pl.ds(me_c * patients + k, 1), :] for k in range(patients)]

    for copy in col_c + dev_c:
        copy.wait_recv()
    products = []
    for k in range(patients):
        blocks = []
        for b in range(VBLOCKS):
            s = k * VBLOCKS + b
            value = None
            for c in range(n_code):
                term = dev_all[c, s].astype(f32) + partials[c][:, rank : rank + 1] * col_all[c, s : s + 1, :]
                value = term if value is None else value + term
            blocks.append(value)
        products.append(jnp.concatenate(blocks, axis=1))
    polars, projected = polar_factors(products, mix_in[...], mine)
    total = functools.reduce(jnp.add, [p * w for p, w in zip(projected, mine)])
    numer_c[me_c] = jnp.concatenate([total[:half], total[half:]], axis=1)
    numer_z = to_code(3, lambda d: numer_c.at[me_c], numer_c.at[me_c])
    for k in range(patients):
        for b in range(VBLOCKS):
            piece = polars[k][:, b * tile_rows : (b + 1) * tile_rows]
            polar_all[me_c, k * VBLOCKS + b] = piece.astype(bf16)
    polar_c = to_code(4, lambda d: polar_all.at[me_c], polar_all.at[me_c])
    for copy in numer_z:
        copy.wait_recv()
    mid[...] = jnp.sum(numer_c[...], axis=0)
    numer_x = to_pat(2, mid, numer_p.at[me_p])
    numer_p[me_p] = mid[...]
    for copy in numer_x:
        copy.wait_recv()
    packed = jnp.sum(numer_p[...], axis=0)
    numer = jnp.concatenate([packed[:, :rank], packed[:, rank:]], axis=0)

    mix = mm(numer, first)
    mix_out[...] = mix
    square = mm(mix, mix, 0, 0)
    terms = jnp.concatenate([jnp.sum(mix * projected[k], axis=0, keepdims=True) for k in range(patients)], axis=0)
    fresh = jnp.maximum(mm(terms, damped_inverse(square * code_gram)), 0.0)
    weight_out[...] = fresh
    row[me_c] = fresh
    row_c = to_code(5, lambda d: row.at[me_c], row.at[me_c])
    for copy in row_c:
        copy.wait_recv()
    row_p = to_pat(3, row, weight_all.at[me_p])
    weight_all[me_p] = row[...]
    for copy in polar_c:
        copy.wait_recv()
    for c in range(n_code):
        for k in range(patients):
            scaled = mix * row[c, k : k + 1, :]
            high = scaled.astype(bf16)
            left = jnp.concatenate([high, (scaled - high.astype(f32)).astype(bf16)], axis=0)
            for b in range(VBLOCKS):
                s = k * VBLOCKS + b
                part = polar_all[c, s]
                spread[c * own + s] = bmm(left, jnp.concatenate([part, part], axis=0), 0, 0).astype(bf16)
    for copy in row_p:
        copy.wait_recv()
    rows = jnp.concatenate(
        [jnp.concatenate([weight_all[p, c] for c in range(n_code)], axis=0) for p in range(n_pat)], axis=0
    )
    inverse[...] = damped_inverse(square * mm(rows, rows, 0, 0))
    for copy in gram_c + col_c + dev_c + old_p + gram_p + numer_z + polar_c + numer_x + row_c + row_p:
        copy.wait_send()


def code_kernel(list_ref, count_ref, visits_ref, tiles, spread, mix, weight, acc, mix_out, weight_out):
    mix_out[...] = mix[...]
    weight_out[...] = weight[...]
    slots, tile_rows, tile_cols = tiles.shape
    rank, codes = acc.shape
    acc[...] = jnp.zeros_like(acc)
    lane_at = lax.broadcasted_iota(jnp.int32, (rank, tile_rows), 1)
    for slot in range(slots):
        segment, code, limit = live_rows(list_ref, count_ref, visits_ref, slot, tile_rows)
        picked = jnp.where(lane_at < limit, spread[segment].astype(f32), 0.0).astype(bf16)
        where = pl.ds(pl.multiple_of(code * tile_cols, tile_cols), tile_cols)
        acc[:, where] += bmm(picked, tiles[slot])


def stacked_inverse(inverse):
    high = inverse.astype(bf16)
    low = (inverse - high.astype(f32)).astype(bf16)
    return jnp.concatenate([high, high, low], axis=1)


def solved_block(left, part):
    top = part.astype(bf16)
    rest = (part - top.astype(f32)).astype(bf16)
    return bmm(left, jnp.concatenate([top, rest, top], axis=0))


def solve_kernel(numer, inverse, result):
    codes = numer.shape[1]
    left = stacked_inverse(inverse[...])
    step = min(2048, codes)
    for start in range(0, codes, step):
        result[:, start : start + step] = solved_block(left, numer[:, start : start + step]).astype(bf16)


def quad_kernel(n_pat, numer, inverse, out, give, keep, pair, send_x, send_y, got_x, got_y, fin, sems, arrive):
    me_p, me_c = lax.axis_index("pat"), lax.axis_index("code")
    core, chip = lax.rem(me_p, 2), me_p // 2
    at_x, at_y = lax.rem(chip, 2), chip // 2
    width = numer.shape[1] // n_pat
    span = width // STREAMS
    part = span // 2
    chips = [chip, at_y * 2 + 1 - at_x, (1 - at_y) * 2 + at_x, (1 - at_y) * 2 + 1 - at_x]
    partner = (chip * 2 + 1 - core, me_c)
    along_x, along_y = (chips[1] * 2 + core, me_c), (chips[2] * 2 + core, me_c)
    copies, tail = [], []
    order = (3, 1, 2, 0)

    def go(src, dst, where):
        n = len(copies)
        copies.append(remote(src, dst, sems.at[n], arrive.at[n], where))
        return copies[-1]

    barrier = pltpu.get_barrier_semaphore()
    for where in (partner, along_x, along_y):
        pl.semaphore_signal(barrier, inc=1, device_id=where, device_id_type=MESH)
    left = stacked_inverse(inverse[...])

    def stream(g):
        def lanes(index, half=None):
            if half is None:
                return pl.ds(pl.multiple_of(index * width + g * span, part), span)
            return pl.ds(pl.multiple_of(index * width + g * span + half * part, part), part)

        pairs = {}
        for s in order:
            give[g, s] = solved_block(left, numer[:, lanes(chips[s] * 2 + 1 - core)]).astype(bf16)
            if g == 0 and s == order[0]:
                pl.semaphore_wait(barrier, 3)
            pairs[s] = go(give.at[g, s], pair.at[g, s], partner)
        yield
        for s in order:
            keep[g, s] = solved_block(left, numer[:, lanes(chips[s] * 2 + core)])
            pairs[s].wait_recv()
            keep[g, s] += pair[g, s].astype(f32)
            if s == 3:
                send_x[g, 0] = keep[g, 3, :, :part].astype(bf16)
                x_far = go(send_x.at[g, 0], got_x.at[g, 0], along_x)
                send_y[g, 0] = keep[g, 3, :, part:].astype(bf16)
                y_far = go(send_y.at[g, 0], got_y.at[g, 0], along_y)
            elif s == 1:
                send_x[g, 1] = keep[g, 1, :, :part].astype(bf16)
                x_near = go(send_x.at[g, 1], got_x.at[g, 1], along_x)
            elif s == 2:
                send_y[g, 1] = keep[g, 2, :, part:].astype(bf16)
                y_near = go(send_y.at[g, 1], got_y.at[g, 1], along_y)
        yield
        x_far.wait_recv()
        send_y[g, 2] = (keep[g, 2, :, :part] + got_x[g, 0].astype(f32)).astype(bf16)
        y_last = go(send_y.at[g, 2], got_y.at[g, 2], along_y)
        y_far.wait_recv()
        send_x[g, 2] = (keep[g, 1, :, part:] + got_y[g, 0].astype(f32)).astype(bf16)
        x_last = go(send_x.at[g, 2], got_x.at[g, 2], along_x)
        yield
        x_near.wait_recv()
        y_last.wait_recv()
        low = keep[g, 0, :, :part] + got_x[g, 1].astype(f32) + got_y[g, 2].astype(f32)
        fin[g, 0] = jnp.maximum(low, 0.0).astype(bf16)
        spots = [out.at[:, lanes(me_p, h)] for h in range(2)]
        x_low = go(fin.at[g, 0], spots[0], along_x)
        y_near.wait_recv()
        x_last.wait_recv()
        high = keep[g, 0, :, part:] + got_y[g, 1].astype(f32) + got_x[g, 2].astype(f32)
        fin[g, 1] = jnp.maximum(high, 0.0).astype(bf16)
        y_high = go(fin.at[g, 1], spots[1], along_y)
        x_high = go(fin.at[g, 1], spots[1], along_x)
        y_low = go(fin.at[g, 0], spots[0], along_y)
        tail.append(go(fin.at[g, 0], spots[0], partner))
        tail.append(go(fin.at[g, 1], spots[1], partner))
        out[:, lanes(me_p, 0)] = fin[g, 0]
        out[:, lanes(me_p, 1)] = fin[g, 1]
        yield

        def pass_on(s, half, where):
            spot = out.at[:, lanes(chips[s] * 2 + core, half)]
            return go(spot, spot, where)

        x_low.wait_recv()
        low_far = pass_on(1, 0, along_y)
        tail.append(pass_on(1, 0, partner))
        y_high.wait_recv()
        high_far = pass_on(2, 1, along_x)
        tail.append(pass_on(2, 1, partner))
        x_high.wait_recv()
        tail.append(pass_on(1, 1, partner))
        y_low.wait_recv()
        tail.append(pass_on(2, 0, partner))
        yield
        low_far.wait_recv()
        tail.append(pass_on(3, 0, partner))
        high_far.wait_recv()
        tail.append(pass_on(3, 1, partner))
        yield

    for _ in zip(*[stream(g) for g in range(STREAMS)]):
        pass
    for copy in tail:
        copy.wait_recv()
    for copy in copies:
        copy.wait_send()


def reduce_kernel(n_pat, y, out, pair, half, got, send_a, recv_a, send_b, recv_b, send_c, recv_c, send_d, recv_d):
    me_p, me_c = lax.axis_index("pat"), lax.axis_index("code")
    chips = n_pat // 2
    chip, core = me_p // 2, lax.rem(me_p, 2)
    width = y.shape[1] // n_pat
    partner = (chip * 2 + 1 - core, me_c)

    def lanes(index):
        return pl.ds(pl.multiple_of(index * width, width), width)

    barrier = pltpu.get_barrier_semaphore()
    pl.semaphore_signal(barrier, inc=1, device_id=partner, device_id_type=MESH)
    for d in range(1, chips):
        pl.semaphore_signal(
            barrier, inc=1, device_id=(lax.rem(chip + d, chips) * 2 + core, me_c), device_id_type=MESH
        )
    pl.semaphore_wait(barrier, chips)

    order = list(range(1, chips)) + [0]
    stage_a, stage_b, stage_c, stage_d = [], [], [], []
    for d in order:
        q = lax.rem(chip + d, chips)
        stage_a.append(
            remote(y.at[:, lanes(q * 2 + 1 - core)], pair.at[d], send_a.at[d], recv_a.at[d], partner)
        )
    mine = None
    for n, d in enumerate(order):
        q = lax.rem(chip + d, chips)
        stage_a[n].wait_recv()
        value = y[:, lanes(q * 2 + core)].astype(f32) + pair[d].astype(f32)
        if d:
            half[d] = value.astype(bf16)
            stage_b.append(remote(half.at[d], got.at[d], send_b.at[d], recv_b.at[d], (q * 2 + core, me_c)))
        else:
            mine = value
    for copy in stage_b:
        copy.wait_recv()
    for d in range(1, chips):
        mine = mine + got[d].astype(f32)
    half[0] = jnp.maximum(mine, 0.0).astype(bf16)
    here = lanes(me_p)
    for d in range(1, chips):
        stage_c.append(
            remote(half.at[0], out.at[:, here], send_c.at[d], recv_c.at[d], (lax.rem(chip + d, chips) * 2 + core, me_c))
        )
    stage_d.append(remote(half.at[0], out.at[:, here], send_d.at[0], recv_d.at[0], partner))
    out[:, here] = half[0]
    for d in range(1, chips):
        stage_c[d - 1].wait_recv()
        q = lax.rem(chip + chips - d, chips)
        spot = out.at[:, lanes(q * 2 + core)]
        stage_d.append(remote(spot, spot, send_d.at[d], recv_d.at[d], partner))
    for copy in stage_d:
        copy.wait_recv()
    for copy in stage_a + stage_b + stage_c + stage_d:
        copy.wait_send()


def dma(*shape):
    return pltpu.SemaphoreType.DMA(shape)


def call(kernel, outs, n_in, scratch=(), smem=0, remote_id=None):
    if remote_id is None:
        params = pltpu.CompilerParams(vmem_limit_bytes=LIMIT)
    else:
        params = pltpu.CompilerParams(vmem_limit_bytes=LIMIT, collective_id=remote_id, has_side_effects=True)
    return pl.pallas_call(
        kernel,
        out_shape=[jax.ShapeDtypeStruct(s, d) for s, d in outs],
        in_specs=[SMEM] * smem + [VMEM] * (n_in - smem),
        out_specs=[VMEM] * len(outs),
        scratch_shapes=list(scratch),
        compiler_params=params,
    )


def body(tile_data, tile_list, tile_count, visit_counts, code_factor_t, visit_mix, patient_weight):
    n_pat, n_code = lax.axis_size("pat"), lax.axis_size("code")
    tiles = tile_data[0, 0]
    listing = jnp.transpose(tile_list[0], (1, 0, 2))
    count = tile_count[0]
    rank, codes = code_factor_t.shape
    slots, tile_rows, tile_cols = tiles.shape
    pat_row = visit_counts.shape[0]
    pat_own = pat_row // n_code
    segments, own = pat_row * VBLOCKS, pat_own * VBLOCKS
    chips = n_pat // 2
    width = codes // n_pat

    dev, col, gram = call(
        products_kernel,
        [((segments, rank, tile_rows), bf16), ((segments, tile_rows), f32), ((n_pat, rank // n_pat, 2 * rank), f32)],
        5,
        [pltpu.VMEM((2 * rank, codes), bf16), pltpu.VMEM((segments, rank, tile_rows), f32)],
        smem=3,
    )(listing, count, visit_counts, tiles, code_factor_t)
    square = ((rank, rank), f32)
    fresh = ((pat_own, rank), f32)
    spread, second, mix_kept, weight_kept = call(
        functools.partial(core_kernel, n_pat, n_code),
        [((segments, rank, tile_rows), bf16), square, square, fresh],
        5,
        [
            pltpu.VMEM((n_code, own, rank, tile_rows), bf16),
            pltpu.VMEM((n_code, own, tile_rows), f32),
            pltpu.VMEM((n_pat, n_code, rank // n_pat, 2 * rank), f32),
            pltpu.VMEM((n_pat, pat_row, rank), f32),
            pltpu.VMEM((n_code, rank // 2, 2 * rank), f32),
            pltpu.VMEM((n_pat, rank // 2, 2 * rank), f32),
            pltpu.VMEM((rank // 2, 2 * rank), f32),
            pltpu.VMEM((n_code, own, rank, tile_rows), bf16),
            pltpu.VMEM((n_code, pat_own, rank), f32),
            pltpu.VMEM((n_pat, n_code, pat_own, rank), f32),
            dma(6, n_code),
            dma(6, n_code),
            dma(4, n_pat),
            dma(4, n_pat),
        ],
        remote_id=1,
    )(dev, col, gram, patient_weight, visit_mix)
    code_numer, mix_new, weight_new = call(code_kernel, [((rank, codes), f32), square, fresh], 7, smem=3)(
        listing, count, visit_counts, tiles, spread, mix_kept, weight_kept
    )
    if chips == 4:
        span = width // STREAMS
        (code_new,) = call(
            functools.partial(quad_kernel, n_pat),
            [((rank, codes), bf16)],
            2,
            [
                pltpu.VMEM((STREAMS, chips, rank, span), bf16),
                pltpu.VMEM((STREAMS, chips, rank, span), f32),
                pltpu.VMEM((STREAMS, chips, rank, span), bf16),
                pltpu.VMEM((STREAMS, 3, rank, span // 2), bf16),
                pltpu.VMEM((STREAMS, 3, rank, span // 2), bf16),
                pltpu.VMEM((STREAMS, 3, rank, span // 2), bf16),
                pltpu.VMEM((STREAMS, 3, rank, span // 2), bf16),
                pltpu.VMEM((STREAMS, 2, rank, span // 2), bf16),
                dma(24 * STREAMS),
                dma(24 * STREAMS),
            ],
            remote_id=4,
        )(code_numer, second)
    else:
        (solved,) = call(solve_kernel, [((rank, codes), bf16)], 2)(code_numer, second)
        (code_new,) = call(
            functools.partial(reduce_kernel, n_pat),
            [((rank, codes), bf16)],
            1,
            [pltpu.VMEM((chips, rank, width), bf16)] * 3 + [dma(chips)] * 8,
            remote_id=4,
        )(solved)
    return (code_new.astype(f32), mix_new, weight_new)


def solution(mesh):
    placed = (
        P("pat", "code", None, None, None),
        P("pat", "code", None, None),
        P("pat", "code"),
        P("pat"),
        P(None, "code"),
        P(),
        P("pat", None),
    )
    return jax.shard_map(
        body,
        mesh=mesh,
        in_specs=placed,
        out_specs=(P(None, "code"), P(), P(("pat", "code"), None)),
        check_vma=False,
    )
```

```python
import functools

import jax
import jax.numpy as jnp
from jax import lax
from jax.experimental import pallas as pl
from jax.experimental.pallas import tpu as pltpu
from jax.sharding import PartitionSpec as P

VBLOCKS = 2
NS_STEPS = 8
INVERSE_STEPS = 7
STREAMS = 2
MESH = pl.DeviceIdType.MESH
damping = 0.1
epsilon = 1e-06

f32 = jnp.float32
bf16 = jnp.bfloat16
VMEM = pl.BlockSpec(memory_space=pltpu.VMEM)
SMEM = pl.BlockSpec(memory_space=pltpu.SMEM)
LIMIT = 32 * 1024 * 1024


def mm(left, right, left_dim=1, right_dim=0):
    return lax.dot_general(
        left,
        right,
        (((left_dim,), (right_dim,)), ((), ())),
        precision=lax.Precision.HIGHEST,
        preferred_element_type=f32,
    )


def bmm(left, right, left_dim=1, right_dim=0):
    return lax.dot_general(
        left, right, (((left_dim,), (right_dim,)), ((), ())), preferred_element_type=f32
    )


def damped_inverse(gram):
    size = gram.shape[0]
    row_at = lax.broadcasted_iota(jnp.int32, (size, size), 0)
    lane_at = lax.broadcasted_iota(jnp.int32, (size, size), 1)
    eye = jnp.where(row_at == lane_at, 1.0, 0.0)
    trace = jnp.sum(jnp.sum(gram * eye, axis=1, keepdims=True), axis=0, keepdims=True)
    mean = trace * (1.0 / size)
    unscale = 1.0 / (mean * (0.5 * size + damping))
    a = gram * unscale + eye * (damping / (0.5 * size + damping))
    rest = eye - a
    tau = (size + 2.0 * damping) / size
    x = eye
    for step in range(INVERSE_STEPS):
        twice = 2.0 * tau * tau
        gain = twice / (twice - 1.0)
        if step == 0:
            x, square = x + rest, mm(rest, rest)
        else:
            both = mm(rest, jnp.concatenate([x, rest], axis=1))
            x, square = x + both[:, :size], both[:, size:]
        x = x * gain
        rest = square * gain - eye * (1.0 / (twice - 1.0))
        tau = twice - 1.0
    x = x + mm(x, eye - mm(a, x))
    return x * unscale


def live_rows(list_ref, count_ref, visits_ref, slot, tile_rows):
    owner, block, code = list_ref[0, 0, slot], list_ref[1, 0, slot], list_ref[2, 0, slot]
    limit = jnp.where(slot < count_ref[0], visits_ref[owner] - block * tile_rows, 0)
    return owner * VBLOCKS + block, code, limit


def gram_kernel(factor, high_out, gram, split):
    rank, codes = factor.shape
    step = min(2048, codes)
    total = jnp.zeros((2 * rank, 2 * rank), f32)
    profile = jnp.zeros((rank, 1), f32)
    for start in range(0, codes, step):
        part = factor[:, start : start + step]
        high = part.astype(bf16)
        high_out[:, start : start + step] = high
        split[:rank, start : start + step] = high
        split[rank:, start : start + step] = (part - high.astype(f32)).astype(bf16)
        profile += jnp.sum(part, axis=1, keepdims=True)
        both = split[:, start : start + step]
        total += bmm(both, both, 1, 1)
    profile = profile * (1.0 / codes)
    square = total[:rank, :rank] + total[:rank, rank:] + total[rank:, :rank] + total[rank:, rank:]
    both = jnp.concatenate([square, jnp.broadcast_to(profile, (rank, rank))], axis=1)
    rows = gram.shape[1]
    for p in range(gram.shape[0]):
        gram[p] = both[p * rows : (p + 1) * rows, :]


def products_kernel(list_ref, count_ref, visits_ref, tiles, factor, gram, dev, col, acc):
    slots, tile_rows, tile_cols = tiles.shape
    rank, codes = factor.shape
    profile = jnp.concatenate([gram[p] for p in range(gram.shape[0])], axis=0)[:, rank : rank + 1]
    acc[...] = jnp.zeros_like(acc)
    lane_at = lax.broadcasted_iota(jnp.int32, (rank, tile_rows), 1)
    for slot in range(slots):
        segment, code, limit = live_rows(list_ref, count_ref, visits_ref, slot, tile_rows)
        picked = factor[:, pl.ds(pl.multiple_of(code * tile_cols, tile_cols), tile_cols)]
        contrib = bmm(picked, tiles[slot], 1, 1)
        acc[segment] += jnp.where(lane_at < limit, contrib, 0.0)
    whole = 1.0 / jnp.sum(profile, axis=0, keepdims=True)
    for segment in range(acc.shape[0]):
        value = acc[segment]
        column = jnp.sum(value, axis=0, keepdims=True) * whole
        col[segment : segment + 1, :] = column
        dev[segment] = (value - profile * column).astype(bf16)


def code_peer(me, distance, n_code):
    return lax.rem(me + distance, n_code)


def greet(n_pat, n_code, me_p, me_c):
    barrier = pltpu.get_barrier_semaphore()
    for d in range(1, n_code):
        pl.semaphore_signal(barrier, inc=1, device_id=(me_p, lax.rem(me_c + d, n_code)), device_id_type=MESH)
    for d in range(1, n_pat):
        pl.semaphore_signal(barrier, inc=1, device_id=(lax.rem(me_p + d, n_pat), me_c), device_id_type=MESH)
    pl.semaphore_wait(barrier, n_code + n_pat - 2)


def remote(src, dst, send, recv, where):
    copy = pltpu.make_async_remote_copy(
        src_ref=src, dst_ref=dst, send_sem=send, recv_sem=recv, device_id=where, device_id_type=MESH
    )
    copy.start()
    return copy


def polar_factors(products, mix, mine):
    rank = mix.shape[0]
    row_at = lax.broadcasted_iota(jnp.int32, (rank, rank), 0)
    lane_at = lax.broadcasted_iota(jnp.int32, (rank, rank), 1)
    eye = jnp.where(row_at == lane_at, 1.0, 0.0)
    targets = [mm(mix * w, x) for w, x in zip(mine, products)]
    crosses, grams, scales = [], [], []
    for target, product in zip(targets, products):
        both = mm(target, jnp.concatenate([target, product], axis=0), 1, 1)
        gram = both[:, :rank]
        norm = jnp.sum(jnp.sum(gram * eye, axis=1, keepdims=True), axis=0, keepdims=True) + epsilon
        crosses.append(both[:, rank:])
        grams.append(gram / norm)
        scales.append(1.0 / jnp.sqrt(norm))
    maps = None
    for step in range(NS_STEPS):
        steps = [1.5 * eye - 0.5 * g for g in grams]
        if step == 0:
            maps, halves = steps, [mm(p, g) for p, g in zip(steps, grams)]
        elif step < NS_STEPS - 1:
            wide = [mm(p, jnp.concatenate([g, q], axis=1)) for p, g, q in zip(steps, grams, maps)]
            halves, maps = [w[:, :rank] for w in wide], [w[:, rank:] for w in wide]
        else:
            maps = [mm(p, q) for p, q in zip(steps, maps)]
        if step < NS_STEPS - 1:
            grams = [mm(h, p) for h, p in zip(halves, steps)]
    maps = [q * scale for q, scale in zip(maps, scales)]
    polars = [mm(q, target) for q, target in zip(maps, targets)]
    return polars, [mm(q, cross) for q, cross in zip(maps, crosses)]


def core_kernel(
    n_pat,
    n_code,
    dev,
    col,
    gram,
    weight,
    mix_in,
    spread,
    inverse,
    mix_out,
    weight_out,
    dev_all,
    col_all,
    gram_all,
    old_all,
    numer_c,
    numer_p,
    mid,
    polar_all,
    row,
    weight_all,
    send_c,
    recv_c,
    send_p,
    recv_p,
):
    me_p, me_c = lax.axis_index("pat"), lax.axis_index("code")
    segments, rank, tile_rows = dev.shape
    own = segments // n_code
    patients = own // VBLOCKS
    half = rank // 2

    def to_code(kind, src, dst):
        copies = []
        for d in range(n_code - 1, 0, -1):
            where = (me_p, lax.rem(me_c + d, n_code))
            copies.append(remote(src(d), dst, send_c.at[kind, d], recv_c.at[kind, d], where))
        return copies

    def to_pat(kind, src, dst):
        copies = []
        for d in range(1, n_pat):
            where = (lax.rem(me_p + d, n_pat), me_c)
            copies.append(remote(src, dst, send_p.at[kind, d], recv_p.at[kind, d], where))
        return copies

    def share(d):
        return pl.ds(lax.rem(me_c + d, n_code) * own, own)

    greet(n_pat, n_code, me_p, me_c)
    gram_c = to_code(0, lambda d: gram.at[me_p], gram_all.at[me_p, me_c])
    col_c = to_code(1, lambda d: col.at[share(d)], col_all.at[me_c])
    dev_c = to_code(2, lambda d: dev.at[share(d)], dev_all.at[me_c])
    old_p = to_pat(0, weight, old_all.at[me_p])
    gram_all[me_p, me_c] = gram[me_p]
    old_all[me_p] = weight[...]
    col_all[me_c] = col[share(0)]
    dev_all[me_c] = dev[share(0)]
    for copy in gram_c:
        copy.wait_recv()
    gram_p = to_pat(1, gram_all.at[me_p], gram_all.at[me_p])
    for copy in old_p + gram_p:
        copy.wait_recv()
    partials = [jnp.concatenate([gram_all[p, c] for p in range(n_pat)], axis=0) for c in range(n_code)]
    code_gram = functools.reduce(jnp.add, partials)[:, :rank]
    olds = old_all[...].reshape(-1, rank)
    first = damped_inverse(code_gram * mm(olds, olds, 0, 0))
    mine = [weight[pl.ds(me_c * patients + k, 1), :] for k in range(patients)]

    for copy in col_c + dev_c:
        copy.wait_recv()
    products = []
    for k in range(patients):
        blocks = []
        for b in range(VBLOCKS):
            s = k * VBLOCKS + b
            value = None
            for c in range(n_code):
                term = dev_all[c, s].astype(f32) + partials[c][:, rank : rank + 1] * col_all[c, s : s + 1, :]
                value = term if value is None else value + term
            blocks.append(value)
        products.append(jnp.concatenate(blocks, axis=1))
    polars, projected = polar_factors(products, mix_in[...], mine)
    total = functools.reduce(jnp.add, [p * w for p, w in zip(projected, mine)])
    numer_c[me_c] = jnp.concatenate([total[:half], total[half:]], axis=1)
    numer_z = to_code(3, lambda d: numer_c.at[me_c], numer_c.at[me_c])
    for k in range(patients):
        for b in range(VBLOCKS):
            piece = polars[k][:, b * tile_rows : (b + 1) * tile_rows]
            polar_all[me_c, k * VBLOCKS + b] = piece.astype(bf16)
    polar_c = to_code(4, lambda d: polar_all.at[me_c], polar_all.at[me_c])
    for copy in numer_z:
        copy.wait_recv()
    mid[...] = jnp.sum(numer_c[...], axis=0)
    numer_x = to_pat(2, mid, numer_p.at[me_p])
    numer_p[me_p] = mid[...]
    for copy in numer_x:
        copy.wait_recv()
    packed = jnp.sum(numer_p[...], axis=0)
    numer = jnp.concatenate([packed[:, :rank], packed[:, rank:]], axis=0)

    mix = mm(numer, first)
    mix_out[...] = mix
    square = mm(mix, mix, 0, 0)
    terms = jnp.concatenate([jnp.sum(mix * projected[k], axis=0, keepdims=True) for k in range(patients)], axis=0)
    fresh = jnp.maximum(mm(terms, damped_inverse(square * code_gram)), 0.0)
    weight_out[...] = fresh
    row[me_c] = fresh
    row_c = to_code(5, lambda d: row.at[me_c], row.at[me_c])
    for copy in row_c:
        copy.wait_recv()
    row_p = to_pat(3, row, weight_all.at[me_p])
    weight_all[me_p] = row[...]
    for copy in polar_c:
        copy.wait_recv()
    for c in range(n_code):
        for k in range(patients):
            scaled = mix * row[c, k : k + 1, :]
            high = scaled.astype(bf16)
            left = jnp.concatenate([high, (scaled - high.astype(f32)).astype(bf16)], axis=0)
            for b in range(VBLOCKS):
                s = k * VBLOCKS + b
                part = polar_all[c, s]
                spread[c * own + s] = bmm(left, jnp.concatenate([part, part], axis=0), 0, 0).astype(bf16)
    for copy in row_p:
        copy.wait_recv()
    rows = jnp.concatenate(
        [jnp.concatenate([weight_all[p, c] for c in range(n_code)], axis=0) for p in range(n_pat)], axis=0
    )
    inverse[...] = damped_inverse(square * mm(rows, rows, 0, 0))
    for copy in gram_c + col_c + dev_c + old_p + gram_p + numer_z + polar_c + numer_x + row_c + row_p:
        copy.wait_send()


def code_kernel(list_ref, count_ref, visits_ref, tiles, spread, mix, weight, acc, mix_out, weight_out):
    mix_out[...] = mix[...]
    weight_out[...] = weight[...]
    slots, tile_rows, tile_cols = tiles.shape
    rank, codes = acc.shape
    acc[...] = jnp.zeros_like(acc)
    lane_at = lax.broadcasted_iota(jnp.int32, (rank, tile_rows), 1)
    for slot in range(slots):
        segment, code, limit = live_rows(list_ref, count_ref, visits_ref, slot, tile_rows)
        picked = jnp.where(lane_at < limit, spread[segment].astype(f32), 0.0).astype(bf16)
        where = pl.ds(pl.multiple_of(code * tile_cols, tile_cols), tile_cols)
        acc[:, where] += bmm(picked, tiles[slot])


def stacked_inverse(inverse):
    high = inverse.astype(bf16)
    low = (inverse - high.astype(f32)).astype(bf16)
    return jnp.concatenate([high, high, low], axis=1)


def solved_block(left, part):
    top = part.astype(bf16)
    rest = (part - top.astype(f32)).astype(bf16)
    return bmm(left, jnp.concatenate([top, rest, top], axis=0))


def solve_kernel(numer, inverse, result):
    codes = numer.shape[1]
    left = stacked_inverse(inverse[...])
    step = min(2048, codes)
    for start in range(0, codes, step):
        result[:, start : start + step] = solved_block(left, numer[:, start : start + step]).astype(bf16)


def quad_kernel(n_pat, numer, inverse, out, give, keep, pair, send_x, send_y, got_x, got_y, fin, sems, arrive):
    me_p, me_c = lax.axis_index("pat"), lax.axis_index("code")
    core, chip = lax.rem(me_p, 2), me_p // 2
    at_x, at_y = lax.rem(chip, 2), chip // 2
    width = numer.shape[1] // n_pat
    span = width // STREAMS
    part = span // 2
    chips = [chip, at_y * 2 + 1 - at_x, (1 - at_y) * 2 + at_x, (1 - at_y) * 2 + 1 - at_x]
    partner = (chip * 2 + 1 - core, me_c)
    along_x, along_y = (chips[1] * 2 + core, me_c), (chips[2] * 2 + core, me_c)
    copies, tail = [], []
    order = (3, 1, 2, 0)

    def go(src, dst, where):
        n = len(copies)
        copies.append(remote(src, dst, sems.at[n], arrive.at[n], where))
        return copies[-1]

    barrier = pltpu.get_barrier_semaphore()
    for where in (partner, along_x, along_y):
        pl.semaphore_signal(barrier, inc=1, device_id=where, device_id_type=MESH)
    left = stacked_inverse(inverse[...])

    def stream(g):
        def lanes(index, half=None):
            if half is None:
                return pl.ds(pl.multiple_of(index * width + g * span, part), span)
            return pl.ds(pl.multiple_of(index * width + g * span + half * part, part), part)

        pairs = {}
        for s in order:
            give[g, s] = solved_block(left, numer[:, lanes(chips[s] * 2 + 1 - core)]).astype(bf16)
            if g == 0 and s == order[0]:
                pl.semaphore_wait(barrier, 3)
            pairs[s] = go(give.at[g, s], pair.at[g, s], partner)
        yield
        for s in order:
            keep[g, s] = solved_block(left, numer[:, lanes(chips[s] * 2 + core)])
            pairs[s].wait_recv()
            keep[g, s] += pair[g, s].astype(f32)
            if s == 3:
                send_x[g, 0] = keep[g, 3, :, :part].astype(bf16)
                x_far = go(send_x.at[g, 0], got_x.at[g, 0], along_x)
                send_y[g, 0] = keep[g, 3, :, part:].astype(bf16)
                y_far = go(send_y.at[g, 0], got_y.at[g, 0], along_y)
            elif s == 1:
                send_x[g, 1] = keep[g, 1, :, :part].astype(bf16)
                x_near = go(send_x.at[g, 1], got_x.at[g, 1], along_x)
            elif s == 2:
                send_y[g, 1] = keep[g, 2, :, part:].astype(bf16)
                y_near = go(send_y.at[g, 1], got_y.at[g, 1], along_y)
        yield
        x_far.wait_recv()
        send_y[g, 2] = (keep[g, 2, :, :part] + got_x[g, 0].astype(f32)).astype(bf16)
        y_last = go(send_y.at[g, 2], got_y.at[g, 2], along_y)
        y_far.wait_recv()
        send_x[g, 2] = (keep[g, 1, :, part:] + got_y[g, 0].astype(f32)).astype(bf16)
        x_last = go(send_x.at[g, 2], got_x.at[g, 2], along_x)
        yield
        x_near.wait_recv()
        y_last.wait_recv()
        low = keep[g, 0, :, :part] + got_x[g, 1].astype(f32) + got_y[g, 2].astype(f32)
        fin[g, 0] = jnp.maximum(low, 0.0).astype(bf16)
        spots = [out.at[:, lanes(me_p, h)] for h in range(2)]
        x_low = go(fin.at[g, 0], spots[0], along_x)
        y_near.wait_recv()
        x_last.wait_recv()
        high = keep[g, 0, :, part:] + got_y[g, 1].astype(f32) + got_x[g, 2].astype(f32)
        fin[g, 1] = jnp.maximum(high, 0.0).astype(bf16)
        y_high = go(fin.at[g, 1], spots[1], along_y)
        x_high = go(fin.at[g, 1], spots[1], along_x)
        y_low = go(fin.at[g, 0], spots[0], along_y)
        tail.append(go(fin.at[g, 0], spots[0], partner))
        tail.append(go(fin.at[g, 1], spots[1], partner))
        out[:, lanes(me_p, 0)] = fin[g, 0]
        out[:, lanes(me_p, 1)] = fin[g, 1]
        yield

        def pass_on(s, half, where):
            spot = out.at[:, lanes(chips[s] * 2 + core, half)]
            return go(spot, spot, where)

        x_low.wait_recv()
        low_far = pass_on(1, 0, along_y)
        tail.append(pass_on(1, 0, partner))
        y_high.wait_recv()
        high_far = pass_on(2, 1, along_x)
        tail.append(pass_on(2, 1, partner))
        x_high.wait_recv()
        tail.append(pass_on(1, 1, partner))
        y_low.wait_recv()
        tail.append(pass_on(2, 0, partner))
        yield
        low_far.wait_recv()
        tail.append(pass_on(3, 0, partner))
        high_far.wait_recv()
        tail.append(pass_on(3, 1, partner))
        yield

    for _ in zip(*[stream(g) for g in range(STREAMS)]):
        pass
    for copy in tail:
        copy.wait_recv()
    for copy in copies:
        copy.wait_send()


def reduce_kernel(n_pat, y, out, pair, half, got, send_a, recv_a, send_b, recv_b, send_c, recv_c, send_d, recv_d):
    me_p, me_c = lax.axis_index("pat"), lax.axis_index("code")
    chips = n_pat // 2
    chip, core = me_p // 2, lax.rem(me_p, 2)
    width = y.shape[1] // n_pat
    partner = (chip * 2 + 1 - core, me_c)

    def lanes(index):
        return pl.ds(pl.multiple_of(index * width, width), width)

    barrier = pltpu.get_barrier_semaphore()
    pl.semaphore_signal(barrier, inc=1, device_id=partner, device_id_type=MESH)
    for d in range(1, chips):
        pl.semaphore_signal(
            barrier, inc=1, device_id=(lax.rem(chip + d, chips) * 2 + core, me_c), device_id_type=MESH
        )
    pl.semaphore_wait(barrier, chips)

    order = list(range(1, chips)) + [0]
    stage_a, stage_b, stage_c, stage_d = [], [], [], []
    for d in order:
        q = lax.rem(chip + d, chips)
        stage_a.append(
            remote(y.at[:, lanes(q * 2 + 1 - core)], pair.at[d], send_a.at[d], recv_a.at[d], partner)
        )
    mine = None
    for n, d in enumerate(order):
        q = lax.rem(chip + d, chips)
        stage_a[n].wait_recv()
        value = y[:, lanes(q * 2 + core)].astype(f32) + pair[d].astype(f32)
        if d:
            half[d] = value.astype(bf16)
            stage_b.append(remote(half.at[d], got.at[d], send_b.at[d], recv_b.at[d], (q * 2 + core, me_c)))
        else:
            mine = value
    for copy in stage_b:
        copy.wait_recv()
    for d in range(1, chips):
        mine = mine + got[d].astype(f32)
    half[0] = jnp.maximum(mine, 0.0).astype(bf16)
    here = lanes(me_p)
    for d in range(1, chips):
        stage_c.append(
            remote(half.at[0], out.at[:, here], send_c.at[d], recv_c.at[d], (lax.rem(chip + d, chips) * 2 + core, me_c))
        )
    stage_d.append(remote(half.at[0], out.at[:, here], send_d.at[0], recv_d.at[0], partner))
    out[:, here] = half[0]
    for d in range(1, chips):
        stage_c[d - 1].wait_recv()
        q = lax.rem(chip + chips - d, chips)
        spot = out.at[:, lanes(q * 2 + core)]
        stage_d.append(remote(spot, spot, send_d.at[d], recv_d.at[d], partner))
    for copy in stage_d:
        copy.wait_recv()
    for copy in stage_a + stage_b + stage_c + stage_d:
        copy.wait_send()


def dma(*shape):
    return pltpu.SemaphoreType.DMA(shape)


def call(kernel, outs, n_in, scratch=(), smem=0, remote_id=None):
    if remote_id is None:
        params = pltpu.CompilerParams(vmem_limit_bytes=LIMIT)
    else:
        params = pltpu.CompilerParams(vmem_limit_bytes=LIMIT, collective_id=remote_id, has_side_effects=True)
    return pl.pallas_call(
        kernel,
        out_shape=[jax.ShapeDtypeStruct(s, d) for s, d in outs],
        in_specs=[SMEM] * smem + [VMEM] * (n_in - smem),
        out_specs=[VMEM] * len(outs),
        scratch_shapes=list(scratch),
        compiler_params=params,
    )


def body(tile_data, tile_list, tile_count, visit_counts, code_factor_t, visit_mix, patient_weight):
    n_pat, n_code = lax.axis_size("pat"), lax.axis_size("code")
    tiles = tile_data[0, 0]
    listing = jnp.transpose(tile_list[0], (1, 0, 2))
    count = tile_count[0]
    rank, codes = code_factor_t.shape
    slots, tile_rows, tile_cols = tiles.shape
    pat_row = visit_counts.shape[0]
    pat_own = pat_row // n_code
    segments, own = pat_row * VBLOCKS, pat_own * VBLOCKS
    chips = n_pat // 2
    width = codes // n_pat

    high, gram = call(
        gram_kernel,
        [((rank, codes), bf16), ((n_pat, rank // n_pat, 2 * rank), f32)],
        1,
        [pltpu.VMEM((2 * rank, codes), bf16)],
    )(code_factor_t)
    dev, col = call(
        products_kernel,
        [((segments, rank, tile_rows), bf16), ((segments, tile_rows), f32)],
        6,
        [pltpu.VMEM((segments, rank, tile_rows), f32)],
        smem=3,
    )(listing, count, visit_counts, tiles, high, gram)
    square = ((rank, rank), f32)
    fresh = ((pat_own, rank), f32)
    spread, second, mix_kept, weight_kept = call(
        functools.partial(core_kernel, n_pat, n_code),
        [((segments, rank, tile_rows), bf16), square, square, fresh],
        5,
        [
            pltpu.VMEM((n_code, own, rank, tile_rows), bf16),
            pltpu.VMEM((n_code, own, tile_rows), f32),
            pltpu.VMEM((n_pat, n_code, rank // n_pat, 2 * rank), f32),
            pltpu.VMEM((n_pat, pat_row, rank), f32),
            pltpu.VMEM((n_code, rank // 2, 2 * rank), f32),
            pltpu.VMEM((n_pat, rank // 2, 2 * rank), f32),
            pltpu.VMEM((rank // 2, 2 * rank), f32),
            pltpu.VMEM((n_code, own, rank, tile_rows), bf16),
            pltpu.VMEM((n_code, pat_own, rank), f32),
            pltpu.VMEM((n_pat, n_code, pat_own, rank), f32),
            dma(6, n_code),
            dma(6, n_code),
            dma(4, n_pat),
            dma(4, n_pat),
        ],
        remote_id=1,
    )(dev, col, gram, patient_weight, visit_mix)
    code_numer, mix_new, weight_new = call(code_kernel, [((rank, codes), f32), square, fresh], 7, smem=3)(
        listing, count, visit_counts, tiles, spread, mix_kept, weight_kept
    )
    if chips == 4:
        span = width // STREAMS
        (code_new,) = call(
            functools.partial(quad_kernel, n_pat),
            [((rank, codes), bf16)],
            2,
            [
                pltpu.VMEM((STREAMS, chips, rank, span), bf16),
                pltpu.VMEM((STREAMS, chips, rank, span), f32),
                pltpu.VMEM((STREAMS, chips, rank, span), bf16),
                pltpu.VMEM((STREAMS, 3, rank, span // 2), bf16),
                pltpu.VMEM((STREAMS, 3, rank, span // 2), bf16),
                pltpu.VMEM((STREAMS, 3, rank, span // 2), bf16),
                pltpu.VMEM((STREAMS, 3, rank, span // 2), bf16),
                pltpu.VMEM((STREAMS, 2, rank, span // 2), bf16),
                dma(24 * STREAMS),
                dma(24 * STREAMS),
            ],
            remote_id=4,
        )(code_numer, second)
    else:
        (solved,) = call(solve_kernel, [((rank, codes), bf16)], 2)(code_numer, second)
        (code_new,) = call(
            functools.partial(reduce_kernel, n_pat),
            [((rank, codes), bf16)],
            1,
            [pltpu.VMEM((chips, rank, width), bf16)] * 3 + [dma(chips)] * 8,
            remote_id=4,
        )(solved)
    return (code_new.astype(f32), mix_new, weight_new)


def solution(mesh):
    placed = (
        P("pat", "code", None, None, None),
        P("pat", "code", None, None),
        P("pat", "code"),
        P("pat"),
        P(None, "code"),
        P(),
        P("pat", None),
    )
    return jax.shard_map(
        body,
        mesh=mesh,
        in_specs=placed,
        out_specs=(P(None, "code"), P(), P(("pat", "code"), None)),
        check_vma=False,
    )
```
